32 devices in a mesh: src: 4 (over y, x), tgt: 8 (over z, core).
Axes of the slice: x: 2, y: 2, z: 4, core: 2. Of those that a mesh axis runs over, the one named last changes fastest.
Arguments:
- pcs_source: bfloat16 [30, 8192], P(None, 'src'), may hold values from -6 to 10
- pcs_target: bfloat16 [30, 16384], P(None, 'tgt'), may hold values from -6 to 6
- growth: float32 [8192], P('src'), may hold values from 0.25 to 4
- scores: bfloat16 [8192, 128], P('src'), may hold values from -6 to 6
Outputs:
- source_potential: float32 [8192], P('src')
- target_potential: float32 [16384], P('tgt')
- transported: float32 [16384, 128], P('tgt')
The draws below stay inside these ranges and needn't reach their ends.
All inputs are finite; a program needn't handle non-finite values.
Results may differ from the reference program's by a relative error of at most 0.0029.
Values sent between devices are 32-bit elements; how exact they have to be, the bound alone decides.
A program may use at most 64 MiB of HBM per device.

```python
import math
import jax
import jax.numpy as jnp
from jax import lax

PCS = 30
PROG = 128
ITERS = 2
NS = 8192
NT = 16384


def draw_pcs_source(key, part):
    base = jnp.clip(jax.random.normal(key, (PCS, NS), jnp.float32), -6.0, 6.0)
    return base.astype(jnp.bfloat16)


def shard_levels(key, dims, cuts, low, top_value):
    def one(dim, shards_of):
        draws = jax.random.uniform(jax.random.fold_in(jax.random.fold_in(key, 6), dim), (shards_of,), jnp.float32, low / len(cuts), top_value / len(cuts))
        return jnp.repeat(jnp.exp(draws), dims[dim] // shards_of).reshape((-1,) + (1,) * (len(dims) - dim - 1))

    level = one(*cuts[0])
    for cut in cuts[1:]:
        level = level * one(*cut)
    return level


def scatter_about(key, dims, deviation, limit, cuts=(), held_as=jnp.bfloat16):
    values = jax.random.normal(key, dims, jnp.float32) * deviation
    if len(cuts) > 0:
        values = shard_levels(key, dims, cuts, -0.22, 0.18) * values
    return jnp.clip(values, min=-limit, max=limit).astype(held_as)


def setup_inputs(seed: int = 0) -> dict:
    arg_keys = jax.random.split(jax.random.key(seed), 5)
    return {
        "pcs_source": draw_pcs_source(jax.random.fold_in(arg_keys[4], 71), 0),
        "pcs_target": scatter_about(arg_keys[1], (PCS, NT), 1.0, 6.0, ((1, 8),)),
        "growth": jnp.clip(jnp.exp(math.log(4.0) - 2.7725887 * jax.random.uniform(arg_keys[2], (NS,), jnp.float32) ** shard_levels(arg_keys[2], (NS,), ((0, 4),), -0.2, 0.2)), 0.25, 4.0),
        "scores": scatter_about(arg_keys[3], (NS, PROG), 1.0, 6.0, ((0, 4),)),
    }


EPSILON = 0.05
MARGIN = 1.0
FACTOR = MARGIN / (MARGIN + EPSILON)


def cost_tile(left, right):
    cross = lax.dot_general(left, right, (((0,), (0,)), ((), ())), preferred_element_type=jnp.float32)
    left_wide = left.astype(jnp.float32)
    right_wide = right.astype(jnp.float32)
    left_sq = jnp.sum(left_wide * left_wide, axis=0)
    right_sq = jnp.sum(right_wide * right_wide, axis=0)
    return (left_sq[:, None] + right_sq[None, :] - 2.0 * cross) / left.shape[0]


def stacked(coords, width):
    return jnp.transpose(coords.reshape(coords.shape[0], -1, width), (1, 0, 2))


def log_sum_rows(logits):
    peak = jnp.max(logits, axis=1)
    return peak + jnp.log(jnp.sum(jnp.exp(logits - peak[:, None]), axis=1))


def reference(pcs_source, pcs_target, growth, scores):
    total_sources = pcs_source.shape[1]
    total_targets = pcs_target.shape[1]
    source_width = math.gcd(total_sources, 256)
    target_width = math.gcd(total_targets, 256)
    source_blocks = stacked(pcs_source, source_width)
    target_blocks = stacked(pcs_target, target_width)
    log_a = jnp.log(growth) - jnp.log(jnp.float32(total_sources))
    log_b = -jnp.log(jnp.float32(total_targets))
    source_potential = jnp.zeros((total_sources,), jnp.float32)
    target_potential = jnp.zeros((total_targets,), jnp.float32)
    for step in range(ITERS):
        gpot = target_potential
        rows = lax.map(lambda block: log_sum_rows((gpot[None, :] - cost_tile(block, pcs_target)) / EPSILON), source_blocks).reshape(-1)
        source_potential = FACTOR * (EPSILON * log_a - EPSILON * rows)
        fpot = source_potential
        columns = lax.map(lambda block: log_sum_rows((fpot[None, :] - cost_tile(block, pcs_source)) / EPSILON), target_blocks).reshape(-1)
        target_potential = FACTOR * (EPSILON * log_b - EPSILON * columns)

    def carry_block(pair):
        block, gblock = pair
        tile = cost_tile(block, pcs_source)
        plan = jnp.exp((source_potential[None, :] + gblock[:, None] - tile) / EPSILON)
        mass = jnp.sum(plan, axis=1)
        carried = jnp.dot(plan.astype(jnp.bfloat16), scores, preferred_element_type=jnp.float32)
        return carried / mass[:, None]

    transported = lax.map(carry_block, (target_blocks, target_potential.reshape(-1, target_width))).reshape(total_targets, -1)
    return source_potential, target_potential, transported
```

```python
import functools
import math

import jax
import jax.numpy as jnp
from jax import lax
from jax.experimental import pallas as pl
from jax.experimental.pallas import tpu as pltpu
from jax.sharding import PartitionSpec as P

ITERS = 2
EPSILON = 0.05
MARGIN = 1.0
FACTOR = MARGIN / (MARGIN + EPSILON)
LANES = 128
LOG2E = math.log2(math.e)
UNIT = EPSILON / LOG2E
MESH = pl.DeviceIdType.MESH
WIDTH, STEP, SUB = 512, 256, 64


def split3(value):
    high = value.astype(jnp.bfloat16).astype(jnp.float32)
    mid = (value - high).astype(jnp.bfloat16).astype(jnp.float32)
    return high, mid, value - high - mid


def depth_of(pcs):
    base = -(-pcs // 8) * 8
    return base, -(-(3 * base + 16) // LANES) * LANES


def augment(coords_ref, wide_ref, columns_ref, scale, source):
    pcs, cells = coords_ref.shape
    base, depth = depth_of(pcs)
    wide = coords_ref[...].astype(jnp.float32)
    norm = -0.5 * scale * jnp.sum(wide * wide, axis=0, keepdims=True)
    at = lax.broadcasted_iota(jnp.int32, (16, cells), 0) - (0 if source else 3)
    high, mid, low = split3(norm)
    extra = jnp.where(at == 0, high, jnp.where(at == 1, mid, jnp.where(at == 2, low, 0.0)))
    at = lax.broadcasted_iota(jnp.int32, (16, cells), 0)
    ones = ((at >= 3) & (at < 6)) | ((at >= 11) & (at < 14)) if source else (at < 3) | ((at >= 8) & (at < 11))
    wide_ref[...] = jnp.zeros(wide_ref.shape, jnp.float32)
    for k, piece in enumerate(split3(scale * wide) if source else (wide,) * 3):
        wide_ref[k * base : k * base + pcs, :] = piece
    wide_ref[3 * base : 3 * base + 16, :] = jnp.where(ones, 1.0, extra)
    columns_ref[...] = wide_ref[...].astype(jnp.bfloat16)


def turn(wide_ref, rows_ref):
    depth, cells = wide_ref.shape
    for k in range(cells // LANES):
        cut = slice(k * LANES, (k + 1) * LANES)
        for d in range(depth // LANES):
            deep = slice(d * LANES, (d + 1) * LANES)
            rows_ref[cut, deep] = wide_ref[deep, cut].T.astype(jnp.bfloat16)


def set_bias(dense, wide_ref, rows_ref, at):
    for p, piece in enumerate(split3(dense)):
        for k in range(dense.shape[0]):
            wide_ref[at + p : at + p + 1, k * LANES : (k + 1) * LANES] = piece[k : k + 1, :]
    turn(wide_ref, rows_ref)


def join(peak, total, block):
    t = block.reshape(-1, 8, LANES)
    newpeak = jnp.maximum(peak, jnp.max(t, axis=0))
    total = total * jnp.exp2(peak - newpeak) + jnp.sum(jnp.exp2(t - newpeak[None]), axis=0)
    return newpeak, total


def closed(peak, total):
    top = jnp.max(peak, axis=0, keepdims=True)
    return top, jnp.sum(total * jnp.exp2(peak - top), axis=0, keepdims=True)


def lse_pass(rows_ref, columns_ref, lse_ref):
    rows, columns = rows_ref.shape[0], columns_ref.shape[1]
    width = math.gcd(columns, WIDTH)
    step = math.gcd(rows, STEP)
    sub = math.gcd(step, SUB)
    halves = width // LANES

    def over_columns(c, unused):
        right = columns_ref[:, pl.ds(pl.multiple_of(c * width, width), width)]
        empty = (jnp.full((8, LANES), -jnp.inf, jnp.float32), jnp.zeros((8, LANES), jnp.float32))
        stats = [empty] * halves
        for r in range(rows // step):
            block = jnp.dot(
                rows_ref[r * step : (r + 1) * step, :], right, preferred_element_type=jnp.float32
            )
            for q in range(step // sub):
                for h in range(halves):
                    cut = block[q * sub : (q + 1) * sub, h * LANES : (h + 1) * LANES]
                    stats[h] = join(*stats[h], cut)
        for h in range(halves):
            top, total = closed(*stats[h])
            lse_ref[pl.ds(c * halves + h, 1), :] = top + jnp.log2(total)
        return unused

    lax.fori_loop(0, columns // width, over_columns, 0)


def fill_tile(rows_ref, right, tile_ref):
    rows, width = tile_ref.shape
    step = math.gcd(rows, STEP)
    peak = jnp.full((8, width), -jnp.inf, jnp.float32)
    for r in range(rows // step):
        at = slice(r * step, (r + 1) * step)
        block = jnp.dot(rows_ref[at, :], right, preferred_element_type=jnp.float32)
        tile_ref[at, :] = block
        peak = jnp.maximum(peak, jnp.max(block.reshape(-1, 8, width), axis=0))
    return jnp.max(peak, axis=0, keepdims=True)


def carry_tile(tile_ref, peak, scores_ref, weights):
    rows = tile_ref.shape[0]
    step = math.gcd(rows, STEP)
    for r in range(rows // step):
        at = slice(r * step, (r + 1) * step)
        weights[at, :] = jnp.exp2(tile_ref[at, :] - peak).astype(jnp.bfloat16)
    return jnp.dot(scores_ref[...], weights[...], preferred_element_type=jnp.float32)


def kernel(
    n_src, n_tgt, xs_ref, yt_ref, growth_ref, scores_ref, f_ref, g_ref, out_ref,
    tile, x_wide, y_wide, x_rows, x_cols, y_rows, y_cols, scores_t, weights, partial,
    row_buf, col_buf, stat, received, row_send, row_recv, col_send, col_recv,
    stat_send, stat_recv, part_send, part_recv, out_send, out_recv,
):
    src, tgt = lax.axis_index("src"), lax.axis_index("tgt")
    barrier = pltpu.get_barrier_semaphore()
    for k in range(1, n_src):
        pl.semaphore_signal(
            barrier, inc=1, device_id={"src": lax.rem(src + k, n_src)}, device_id_type=MESH
        )
    for k in range(1, n_tgt):
        pl.semaphore_signal(
            barrier, inc=1, device_id={"tgt": lax.rem(tgt + k, n_tgt)}, device_id_type=MESH
        )

    pcs, rows = xs_ref.shape
    columns = yt_ref.shape[1]
    programs = scores_ref.shape[1]
    scale = 2.0 * LOG2E / (pcs * EPSILON)
    bias_at = 3 * depth_of(pcs)[0] + 8
    augment(yt_ref, y_wide, y_cols, scale, False)
    turn(y_wide, y_rows)
    augment(xs_ref, x_wide, x_cols, scale, True)

    def exchange(buf, axis, me, n, send, recv):
        copies = [
            pltpu.make_async_remote_copy(
                src_ref=buf.at[me], dst_ref=buf.at[me], send_sem=send.at[k], recv_sem=recv.at[k],
                device_id={axis: lax.rem(me + k, n)}, device_id_type=MESH,
            )
            for k in range(1, n)
        ]
        for copy in copies:
            copy.start()
        return copies

    def joined(buf, n):
        parts = [buf[d] for d in range(n)]
        top = functools.reduce(jnp.maximum, parts)
        return top + jnp.log2(sum(jnp.exp2(part - top) for part in parts))

    log_a = jnp.log2(growth_ref[...]) - math.log2(rows * n_src)
    log_b = -math.log2(columns * n_tgt)
    for step in range(ITERS):
        first = step == 0
        lse_pass(y_rows, x_cols, row_buf.at[step, tgt])
        if first:
            pl.semaphore_wait(barrier, n_src + n_tgt - 2)
        copies = exchange(row_buf.at[step], "tgt", tgt, n_tgt, row_send.at[step], row_recv.at[step])
        if first:
            for k in range(rows // LANES):
                cut = slice(k * LANES, (k + 1) * LANES)
                scores_t[0:programs, cut] = scores_ref[cut, :].astype(jnp.float32).T.astype(jnp.bfloat16)
            scores_t[programs:, :] = jnp.ones((16, rows), jnp.bfloat16)
        for copy in copies:
            copy.wait()
        potential = FACTOR * (log_a - joined(row_buf.at[step], n_tgt))
        set_bias(potential, x_wide, x_rows, bias_at)
        if step < ITERS - 1:
            lse_pass(x_rows, y_cols, col_buf.at[step, src])
            copies = exchange(
                col_buf.at[step], "src", src, n_src, col_send.at[step], col_recv.at[step]
            )
            for copy in copies:
                copy.wait()
            set_bias(FACTOR * (log_b - joined(col_buf.at[step], n_src)), y_wide, y_rows, bias_at + 3)
    f_ref[...] = UNIT * potential

    piece = columns // n_src
    width = math.gcd(piece, WIDTH)
    halves = width // LANES
    parts = []

    def fill(unit):
        k, c = divmod(unit, piece // width)
        start = lax.rem(src + k + 1, n_src) * piece + c * width
        start = pl.multiple_of(start, width)
        right = y_cols[:, pl.ds(start, width)]
        return start, fill_tile(x_rows, right, tile.at[unit % 2])

    units = n_src * (piece // width)
    ready = fill(0)
    for unit in range(units):
        start, peak = ready
        if unit + 1 < units:
            ready = fill(unit + 1)
        carried = carry_tile(tile.at[unit % 2], peak, scores_t, weights.at[unit % 2])
        for h in range(halves):
            lanes = slice(h * LANES, (h + 1) * LANES)
            stat[src, 0, pl.ds(start // LANES + h, 1), :] = carried[programs : programs + 1, lanes]
            stat[src, 1, pl.ds(start // LANES + h, 1), :] = peak[:, lanes]
            at = pl.ds(pl.multiple_of(start + h * LANES, LANES), LANES)
            partial[at, :] = carried[0:programs, lanes].T
        k = (unit + 1) * width // piece
        owner = lax.rem(src + k, n_src)
        if (unit + 1) * width % piece:
            continue
        if k < n_src:
            copy = pltpu.make_async_remote_copy(
                src_ref=partial.at[pl.ds(pl.multiple_of(owner * piece, piece), piece), :],
                dst_ref=received.at[k], send_sem=part_send.at[k], recv_sem=part_recv.at[k],
                device_id={"src": owner}, device_id_type=MESH,
            )
            copy.start()
            parts.append(copy)
    copies = exchange(stat, "src", src, n_src, stat_send, stat_recv)
    for copy in copies:
        copy.wait()
    peak = functools.reduce(jnp.maximum, [stat[d, 1] for d in range(n_src)])
    total = sum(stat[d, 0] * jnp.exp2(stat[d, 1] - peak) for d in range(n_src))
    g_ref[...] = UNIT * FACTOR * (log_b - (peak + jnp.log2(total)))
    for d in range(n_src):
        stat[d, 0] = jnp.exp2(stat[d, 1] - peak) / total
    for copy in parts:
        copy.wait()
    first_row = src * (piece // LANES)
    for q in range(piece // LANES):
        mine = pl.ds(pl.multiple_of(src * piece + q * LANES, LANES), LANES)
        result = None
        for k in range(n_src):
            sender = lax.rem(src - k + n_src, n_src)
            share = jnp.broadcast_to(
                stat[sender, 0, pl.ds(first_row + q, 1), :], (LANES, LANES)
            ).T
            block = partial[mine, :] if k == 0 else received[k, q * LANES : (q + 1) * LANES, :]
            result = share * block if result is None else result + share * block
        out_ref[mine, :] = result
    mine = pl.ds(pl.multiple_of(src * piece, piece), piece)
    copies = [
        pltpu.make_async_remote_copy(
            src_ref=out_ref.at[mine, :], dst_ref=out_ref.at[mine, :],
            send_sem=out_send.at[k], recv_sem=out_recv.at[k],
            device_id={"src": lax.rem(src + k, n_src)}, device_id_type=MESH,
        )
        for k in range(1, n_src)
    ]
    for copy in copies:
        copy.start()
    for copy in copies:
        copy.wait()


def solution(mesh):
    n_src, n_tgt = mesh.shape["src"], mesh.shape["tgt"]

    def shards(pcs_source, pcs_target, growth, scores):
        rows, columns = pcs_source.shape[1], pcs_target.shape[1]
        programs = scores.shape[1]
        piece = columns // n_src
        width = math.gcd(piece, WIDTH)
        depth = depth_of(pcs_source.shape[0])[1]
        f32, bf16 = jnp.float32, jnp.bfloat16
        sem = pltpu.SemaphoreType.DMA
        whole = pl.BlockSpec(memory_space=pltpu.VMEM)
        dense_r, dense_c = (rows // LANES, LANES), (columns // LANES, LANES)
        f, g, out = pl.pallas_call(
            functools.partial(kernel, n_src, n_tgt),
            out_shape=(
                jax.ShapeDtypeStruct(dense_r, f32),
                jax.ShapeDtypeStruct(dense_c, f32),
                jax.ShapeDtypeStruct((columns, programs), f32),
            ),
            in_specs=[whole] * 4,
            out_specs=(whole,) * 3,
            scratch_shapes=[
                pltpu.VMEM((2, rows, width), f32),
                pltpu.VMEM((depth, rows), f32),
                pltpu.VMEM((depth, columns), f32),
                pltpu.VMEM((rows, depth), bf16),
                pltpu.VMEM((depth, rows), bf16),
                pltpu.VMEM((columns, depth), bf16),
                pltpu.VMEM((depth, columns), bf16),
                pltpu.VMEM((programs + 16, rows), bf16),
                pltpu.VMEM((2, rows, width), bf16),
                pltpu.VMEM((columns, programs), f32),
                pltpu.VMEM((ITERS, n_tgt) + dense_r, f32),
                pltpu.VMEM((ITERS, n_src) + dense_c, f32),
                pltpu.VMEM((n_src, 2) + dense_c, f32),
                pltpu.VMEM((n_src, piece, programs), f32),
                sem((ITERS, n_tgt)),
                sem((ITERS, n_tgt)),
                sem((ITERS, n_src)),
                sem((ITERS, n_src)),
                sem((n_src,)),
                sem((n_src,)),
                sem((n_src,)),
                sem((n_src,)),
                sem((n_src,)),
                sem((n_src,)),
            ],
            compiler_params=pltpu.CompilerParams(
                collective_id=0, has_side_effects=True, vmem_limit_bytes=60 * 2**20
            ),
            name="coupling",
        )(pcs_source, pcs_target, growth.reshape(dense_r), scores)
        return f.reshape(-1), g.reshape(-1), out

    in_specs = (P(None, "src"), P(None, "tgt"), P("src"), P("src", None))
    out_specs = (P("src"), P("tgt"), P("tgt", None))
    return jax.shard_map(shards, mesh=mesh, in_specs=in_specs, out_specs=out_specs, check_vma=False)
```

```python
import functools
import math

import jax
import jax.numpy as jnp
from jax import lax
from jax.experimental import pallas as pl
from jax.experimental.pallas import tpu as pltpu
from jax.sharding import PartitionSpec as P

ITERS = 2
EPSILON = 0.05
MARGIN = 1.0
FACTOR = MARGIN / (MARGIN + EPSILON)
LANES = 128
LOG2E = math.log2(math.e)
UNIT = EPSILON / LOG2E
MESH = pl.DeviceIdType.MESH
WIDTH, STEP, SUB = 512, 256, 64


def split3(value):
    high = value.astype(jnp.bfloat16).astype(jnp.float32)
    mid = (value - high).astype(jnp.bfloat16).astype(jnp.float32)
    return high, mid, value - high - mid


def depth_of(pcs):
    base = -(-pcs // 8) * 8
    return base, -(-(3 * base + 16) // LANES) * LANES


def augment(coords_ref, wide_ref, columns_ref, scale, source):
    pcs, cells = coords_ref.shape
    base, depth = depth_of(pcs)
    wide = coords_ref[...].astype(jnp.float32)
    norm = -0.5 * scale * jnp.sum(wide * wide, axis=0, keepdims=True)
    at = lax.broadcasted_iota(jnp.int32, (16, cells), 0) - (0 if source else 3)
    high, mid, low = split3(norm)
    extra = jnp.where(at == 0, high, jnp.where(at == 1, mid, jnp.where(at == 2, low, 0.0)))
    at = lax.broadcasted_iota(jnp.int32, (16, cells), 0)
    ones = ((at >= 3) & (at < 6)) | ((at >= 11) & (at < 14)) if source else (at < 3) | ((at >= 8) & (at < 11))
    wide_ref[...] = jnp.zeros(wide_ref.shape, jnp.float32)
    for k, piece in enumerate(split3(scale * wide) if source else (wide,) * 3):
        wide_ref[k * base : k * base + pcs, :] = piece
    wide_ref[3 * base : 3 * base + 16, :] = jnp.where(ones, 1.0, extra)
    columns_ref[...] = wide_ref[...].astype(jnp.bfloat16)


def turn(wide_ref, rows_ref, first, last):
    depth = wide_ref.shape[0]
    for k in range(first // LANES, last // LANES):
        cut = slice(k * LANES, (k + 1) * LANES)
        for d in range(depth // LANES):
            deep = slice(d * LANES, (d + 1) * LANES)
            rows_ref[cut, deep] = wide_ref[deep, cut].T.astype(jnp.bfloat16)


def set_bias(dense, wide_ref, rows_ref, at, first):
    cells = dense.shape[0] * LANES
    for p, piece in enumerate(split3(dense)):
        for k in range(dense.shape[0]):
            lanes = slice(first + k * LANES, first + (k + 1) * LANES)
            wide_ref[at + p : at + p + 1, lanes] = piece[k : k + 1, :]
    turn(wide_ref, rows_ref, first, first + cells)


def halves_of(cells):
    parts = math.gcd(2, max(cells // (8 * LANES), 1))
    return [(p * (cells // parts), (p + 1) * (cells // parts)) for p in range(parts)]


def join(peak, total, block):
    t = block.reshape(-1, 8, LANES)
    newpeak = jnp.maximum(peak, jnp.max(t, axis=0))
    total = total * jnp.exp2(peak - newpeak) + jnp.sum(jnp.exp2(t - newpeak[None]), axis=0)
    return newpeak, total


def closed(peak, total):
    top = jnp.max(peak, axis=0, keepdims=True)
    return top, jnp.sum(total * jnp.exp2(peak - top), axis=0, keepdims=True)


def lse_pass(rows_ref, columns_ref, stats_ref, lse_ref, row_span, lane_span, fresh):
    (low, high), (begin, end) = row_span, lane_span
    width = math.gcd(end - begin, WIDTH)
    step = math.gcd(high - low, STEP)
    sub = math.gcd(step, SUB)
    halves = width // LANES

    def over_columns(c, unused):
        right = columns_ref[:, pl.ds(pl.multiple_of(begin + c * width, width), width)]
        tiles = [begin // LANES + c * halves + h for h in range(halves)]
        if fresh:
            empty = (jnp.full((8, LANES), -jnp.inf, jnp.float32), jnp.zeros((8, LANES), jnp.float32))
            stats = [empty] * halves
        else:
            stats = [(stats_ref[0, tile], stats_ref[1, tile]) for tile in tiles]
        for r in range((high - low) // step):
            block = jnp.dot(
                rows_ref[low + r * step : low + (r + 1) * step, :], right,
                preferred_element_type=jnp.float32,
            )
            for q in range(step // sub):
                for h in range(halves):
                    cut = block[q * sub : (q + 1) * sub, h * LANES : (h + 1) * LANES]
                    stats[h] = join(*stats[h], cut)
        for tile, (peak, total) in zip(tiles, stats):
            if lse_ref is None:
                stats_ref[0, tile] = peak
                stats_ref[1, tile] = total
            else:
                top, total = closed(peak, total)
                lse_ref[pl.ds(tile, 1), :] = top + jnp.log2(total)
        return unused

    lax.fori_loop(0, (end - begin) // width, over_columns, 0)


def fill_tile(rows_ref, right, tile_ref, row_span, peak):
    low, high = row_span
    width = tile_ref.shape[1]
    step = math.gcd(high - low, STEP)
    for r in range((high - low) // step):
        at = slice(low + r * step, low + (r + 1) * step)
        block = jnp.dot(rows_ref[at, :], right, preferred_element_type=jnp.float32)
        tile_ref[at, :] = block
        peak = jnp.maximum(peak, jnp.max(block.reshape(-1, 8, width), axis=0))
    return peak


def carry_tile(tile_ref, peak, scores_ref, weights):
    rows = tile_ref.shape[0]
    step = math.gcd(rows, STEP)
    for r in range(rows // step):
        at = slice(r * step, (r + 1) * step)
        weights[at, :] = jnp.exp2(tile_ref[at, :] - peak).astype(jnp.bfloat16)
    return jnp.dot(scores_ref[...], weights[...], preferred_element_type=jnp.float32)


def kernel(
    n_src, n_tgt, xs_ref, yt_ref, growth_ref, scores_ref, f_ref, g_ref, out_ref,
    tile, x_wide, y_wide, x_rows, x_cols, y_rows, y_cols, scores_t, weights, partial, running,
    row_buf, col_buf, stat, received, row_send, row_recv, col_send, col_recv,
    stat_send, stat_recv, part_send, part_recv, out_send, out_recv,
):
    src, tgt = lax.axis_index("src"), lax.axis_index("tgt")
    barrier = pltpu.get_barrier_semaphore()
    for k in range(1, n_src):
        pl.semaphore_signal(
            barrier, inc=1, device_id={"src": lax.rem(src + k, n_src)}, device_id_type=MESH
        )
    for k in range(1, n_tgt):
        pl.semaphore_signal(
            barrier, inc=1, device_id={"tgt": lax.rem(tgt + k, n_tgt)}, device_id_type=MESH
        )

    pcs, rows = xs_ref.shape
    columns = yt_ref.shape[1]
    programs = scores_ref.shape[1]
    scale = 2.0 * LOG2E / (pcs * EPSILON)
    bias_at = 3 * depth_of(pcs)[0] + 8
    augment(yt_ref, y_wide, y_cols, scale, False)
    turn(y_wide, y_rows, 0, columns)
    augment(xs_ref, x_wide, x_cols, scale, True)

    def exchange(buf, axis, me, n, send, recv, lines):
        copies = [
            pltpu.make_async_remote_copy(
                src_ref=buf.at[me, lines], dst_ref=buf.at[me, lines],
                send_sem=send.at[k], recv_sem=recv.at[k],
                device_id={axis: lax.rem(me + k, n)}, device_id_type=MESH,
            )
            for k in range(1, n)
        ]
        for copy in copies:
            copy.start()
        return copies

    def joined(buf, n, lines):
        parts = [buf[d, lines] for d in range(n)]
        top = functools.reduce(jnp.maximum, parts)
        return top + jnp.log2(sum(jnp.exp2(part - top) for part in parts))

    log_a = jnp.log2(growth_ref[...]) - math.log2(rows * n_src)
    log_b = -math.log2(columns * n_tgt)
    source_halves, target_halves = halves_of(rows), halves_of(columns)

    def lines_of(span):
        return slice(span[0] // LANES, span[1] // LANES)

    def finish(rows_ref, columns_ref, row_span, spans, fresh, buf, axis, me, n, send, recv, enter=False):
        sent = []
        for h, span in enumerate(spans):
            lse_pass(rows_ref, columns_ref, running, buf.at[me], row_span, span, fresh)
            if enter and h == 0:
                pl.semaphore_wait(barrier, n_src + n_tgt - 2)
            sent.append(exchange(buf, axis, me, n, send.at[h], recv.at[h], lines_of(span)))
        return sent

    def settle(copies):
        for copy in copies:
            copy.wait()

    for step in range(ITERS):
        over_tgt = (row_buf.at[step], "tgt", tgt, n_tgt, row_send.at[step], row_recv.at[step])
        over_src = (col_buf.at[step], "src", src, n_src, col_send.at[step], col_recv.at[step])
        if step == 0:
            sent = finish(
                y_rows, x_cols, (0, columns), source_halves, True, *over_tgt, enter=True
            )
            for k in range(rows // LANES):
                cut = slice(k * LANES, (k + 1) * LANES)
                scores_t[0:programs, cut] = scores_ref[cut, :].astype(jnp.float32).T.astype(jnp.bfloat16)
            scores_t[programs:, :] = jnp.ones((16, rows), jnp.bfloat16)
        else:
            for h, span in enumerate(target_halves):
                settle(sent[h])
                lines = lines_of(span)
                g = FACTOR * (log_b - joined(col_buf.at[step - 1], n_src, lines))
                set_bias(g, y_wide, y_rows, bias_at + 3, span[0])
                if h < len(target_halves) - 1:
                    lse_pass(y_rows, x_cols, running, None, span, (0, rows), h == 0)
            sent = finish(y_rows, x_cols, span, source_halves, h == 0, *over_tgt)
        if step == ITERS - 1:
            break
        for h, span in enumerate(source_halves):
            settle(sent[h])
            lines = lines_of(span)
            f = FACTOR * (log_a[lines] - joined(row_buf.at[step], n_tgt, lines))
            set_bias(f, x_wide, x_rows, bias_at, span[0])
            if h < len(source_halves) - 1:
                lse_pass(x_rows, y_cols, running, None, span, (0, columns), h == 0)
        sent = finish(x_rows, y_cols, span, target_halves, h == 0, *over_src)

    piece = columns // n_src
    width = math.gcd(piece, WIDTH)
    halves = width // LANES
    parts = []

    def start_of(unit):
        k, c = divmod(unit, piece // width)
        return pl.multiple_of(lax.rem(src + k + 1, n_src) * piece + c * width, width)

    def fill(unit, span, peak):
        right = y_cols[:, pl.ds(start_of(unit), width)]
        return fill_tile(x_rows, right, tile.at[unit % 2], span, peak)

    units = n_src * (piece // width)
    empty = jnp.full((8, width), -jnp.inf, jnp.float32)
    ready = empty
    for h, span in enumerate(source_halves):
        settle(sent[h])
        lines = lines_of(span)
        f = FACTOR * (log_a[lines] - joined(row_buf.at[ITERS - 1], n_tgt, lines))
        f_ref[lines, :] = UNIT * f
        set_bias(f, x_wide, x_rows, bias_at, span[0])
        ready = fill(0, span, ready)
    for unit in range(units):
        start, peak = start_of(unit), jnp.max(ready, axis=0, keepdims=True)
        if unit + 1 < units:
            ready = fill(unit + 1, (0, rows), empty)
        carried = carry_tile(tile.at[unit % 2], peak, scores_t, weights.at[unit % 2])
        for h in range(halves):
            lanes = slice(h * LANES, (h + 1) * LANES)
            stat[src, 0, pl.ds(start // LANES + h, 1), :] = carried[programs : programs + 1, lanes]
            stat[src, 1, pl.ds(start // LANES + h, 1), :] = peak[:, lanes]
            at = pl.ds(pl.multiple_of(start + h * LANES, LANES), LANES)
            partial[at, :] = carried[0:programs, lanes].T
        k = (unit + 1) * width // piece
        owner = lax.rem(src + k, n_src)
        if (unit + 1) * width % piece:
            continue
        if k < n_src:
            copy = pltpu.make_async_remote_copy(
                src_ref=partial.at[pl.ds(pl.multiple_of(owner * piece, piece), piece), :],
                dst_ref=received.at[k], send_sem=part_send.at[k], recv_sem=part_recv.at[k],
                device_id={"src": owner}, device_id_type=MESH,
            )
            copy.start()
            parts.append(copy)
    copies = exchange(stat, "src", src, n_src, stat_send, stat_recv, slice(0, 2))
    for copy in copies:
        copy.wait()
    peak = functools.reduce(jnp.maximum, [stat[d, 1] for d in range(n_src)])
    total = sum(stat[d, 0] * jnp.exp2(stat[d, 1] - peak) for d in range(n_src))
    g_ref[...] = UNIT * FACTOR * (log_b - (peak + jnp.log2(total)))
    for d in range(n_src):
        stat[d, 0] = jnp.exp2(stat[d, 1] - peak) / total
    for copy in parts:
        copy.wait()
    first_row = src * (piece // LANES)
    for q in range(piece // LANES):
        mine = pl.ds(pl.multiple_of(src * piece + q * LANES, LANES), LANES)
        result = None
        for k in range(n_src):
            sender = lax.rem(src - k + n_src, n_src)
            share = jnp.broadcast_to(
                stat[sender, 0, pl.ds(first_row + q, 1), :], (LANES, LANES)
            ).T
            block = partial[mine, :] if k == 0 else received[k, q * LANES : (q + 1) * LANES, :]
            result = share * block if result is None else result + share * block
        out_ref[mine, :] = result
    mine = pl.ds(pl.multiple_of(src * piece, piece), piece)
    copies = [
        pltpu.make_async_remote_copy(
            src_ref=out_ref.at[mine, :], dst_ref=out_ref.at[mine, :],
            send_sem=out_send.at[k], recv_sem=out_recv.at[k],
            device_id={"src": lax.rem(src + k, n_src)}, device_id_type=MESH,
        )
        for k in range(1, n_src)
    ]
    for copy in copies:
        copy.start()
    for copy in copies:
        copy.wait()


def solution(mesh):
    n_src, n_tgt = mesh.shape["src"], mesh.shape["tgt"]

    def shards(pcs_source, pcs_target, growth, scores):
        rows, columns = pcs_source.shape[1], pcs_target.shape[1]
        programs = scores.shape[1]
        piece = columns // n_src
        width = math.gcd(piece, WIDTH)
        depth = depth_of(pcs_source.shape[0])[1]
        f32, bf16 = jnp.float32, jnp.bfloat16
        sem = pltpu.SemaphoreType.DMA
        whole = pl.BlockSpec(memory_space=pltpu.VMEM)
        dense_r, dense_c = (rows // LANES, LANES), (columns // LANES, LANES)
        f, g, out = pl.pallas_call(
            functools.partial(kernel, n_src, n_tgt),
            out_shape=(
                jax.ShapeDtypeStruct(dense_r, f32),
                jax.ShapeDtypeStruct(dense_c, f32),
                jax.ShapeDtypeStruct((columns, programs), f32),
            ),
            in_specs=[whole] * 4,
            out_specs=(whole,) * 3,
            scratch_shapes=[
                pltpu.VMEM((2, rows, width), f32),
                pltpu.VMEM((depth, rows), f32),
                pltpu.VMEM((depth, columns), f32),
                pltpu.VMEM((rows, depth), bf16),
                pltpu.VMEM((depth, rows), bf16),
                pltpu.VMEM((columns, depth), bf16),
                pltpu.VMEM((depth, columns), bf16),
                pltpu.VMEM((programs + 16, rows), bf16),
                pltpu.VMEM((2, rows, width), bf16),
                pltpu.VMEM((columns, programs), f32),
                pltpu.VMEM((2, max(rows, columns) // LANES, 8, LANES), f32),
                pltpu.VMEM((ITERS, n_tgt) + dense_r, f32),
                pltpu.VMEM((ITERS, n_src) + dense_c, f32),
                pltpu.VMEM((n_src, 2) + dense_c, f32),
                pltpu.VMEM((n_src, piece, programs), f32),
                sem((ITERS, 2, n_tgt)),
                sem((ITERS, 2, n_tgt)),
                sem((ITERS, 2, n_src)),
                sem((ITERS, 2, n_src)),
                sem((n_src,)),
                sem((n_src,)),
                sem((n_src,)),
                sem((n_src,)),
                sem((n_src,)),
                sem((n_src,)),
            ],
            compiler_params=pltpu.CompilerParams(
                collective_id=0, has_side_effects=True, vmem_limit_bytes=60 * 2**20
            ),
            name="coupling",
        )(pcs_source, pcs_target, growth.reshape(dense_r), scores)
        return f.reshape(-1), g.reshape(-1), out

    in_specs = (P(None, "src"), P(None, "tgt"), P("src"), P("src", None))
    out_specs = (P("src"), P("tgt"), P("tgt", None))
    return jax.shard_map(shards, mesh=mesh, in_specs=in_specs, out_specs=out_specs, check_vma=False)
```

```python
import functools
import math

import jax
import jax.numpy as jnp
from jax import lax
from jax.experimental import pallas as pl
from jax.experimental.pallas import tpu as pltpu
from jax.sharding import PartitionSpec as P

ITERS = 2
EPSILON = 0.05
MARGIN = 1.0
FACTOR = MARGIN / (MARGIN + EPSILON)
LANES = 128
LOG2E = math.log2(math.e)
UNIT = EPSILON / LOG2E
MESH = pl.DeviceIdType.MESH
WIDTH, STEP, SUB = 512, 256, 64


def split3(value):
    high = value.astype(jnp.bfloat16).astype(jnp.float32)
    mid = (value - high).astype(jnp.bfloat16).astype(jnp.float32)
    return high, mid, value - high - mid


def depth_of(pcs):
    base = -(-pcs // 8) * 8
    return base, -(-(3 * base + 16) // LANES) * LANES


def augment(coords, wide_ref, scale, source):
    pcs, cells = coords.shape
    base, depth = depth_of(pcs)
    wide = coords.astype(jnp.float32)
    norm = -0.5 * scale * jnp.sum(wide * wide, axis=0, keepdims=True)
    at = lax.broadcasted_iota(jnp.int32, (16, cells), 0) - (0 if source else 3)
    high, mid, low = split3(norm)
    extra = jnp.where(at == 0, high, jnp.where(at == 1, mid, jnp.where(at == 2, low, 0.0)))
    at = lax.broadcasted_iota(jnp.int32, (16, cells), 0)
    ones = ((at >= 3) & (at < 6)) | ((at >= 11) & (at < 14)) if source else (at < 3) | ((at >= 8) & (at < 11))
    wide_ref[...] = jnp.zeros(wide_ref.shape, jnp.float32)
    for k, piece in enumerate(split3(scale * wide) if source else (wide,) * 3):
        wide_ref[k * base : k * base + pcs, :] = piece
    wide_ref[3 * base : 3 * base + 16, :] = jnp.where(ones, 1.0, extra)


def turn(wide_ref, rows_ref, first, last):
    depth = wide_ref.shape[0]
    for k in range(first // LANES, last // LANES):
        cut = slice(k * LANES, (k + 1) * LANES)
        for d in range(depth // LANES):
            deep = slice(d * LANES, (d + 1) * LANES)
            rows_ref[cut, deep] = wide_ref[deep, cut].T.astype(jnp.bfloat16)


def set_bias(dense, wide_ref, rows_ref, at, first):
    cells = dense.shape[0] * LANES
    for p, piece in enumerate(split3(dense)):
        for k in range(dense.shape[0]):
            lanes = slice(first + k * LANES, first + (k + 1) * LANES)
            wide_ref[at + p : at + p + 1, lanes] = piece[k : k + 1, :]
    turn(wide_ref, rows_ref, first, first + cells)


def halves_of(cells):
    parts = math.gcd(2, max(cells // (8 * LANES), 1))
    return [(p * (cells // parts), (p + 1) * (cells // parts)) for p in range(parts)]


def join(peak, total, block):
    t = block.reshape(-1, 8, LANES)
    newpeak = jnp.maximum(peak, jnp.max(t, axis=0))
    total = total * jnp.exp2(peak - newpeak) + jnp.sum(jnp.exp2(t - newpeak[None]), axis=0)
    return newpeak, total


def closed(peak, total):
    top = jnp.max(peak, axis=0, keepdims=True)
    return top, jnp.sum(total * jnp.exp2(peak - top), axis=0, keepdims=True)


def lse_pass(rows_ref, columns_ref, stats_ref, lse_ref, row_span, lane_span, fresh):
    (low, high), (begin, end) = row_span, lane_span
    width = math.gcd(end - begin, WIDTH)
    step = math.gcd(high - low, STEP)
    sub = math.gcd(step, SUB)
    halves = width // LANES

    def over_columns(c, unused):
        right = columns_ref[:, pl.ds(pl.multiple_of(begin + c * width, width), width)]
        tiles = [begin // LANES + c * halves + h for h in range(halves)]
        if fresh:
            empty = (jnp.full((8, LANES), -jnp.inf, jnp.float32), jnp.zeros((8, LANES), jnp.float32))
            stats = [empty] * halves
        else:
            stats = [(stats_ref[0, tile], stats_ref[1, tile]) for tile in tiles]
        for r in range((high - low) // step):
            block = jnp.dot(
                rows_ref[low + r * step : low + (r + 1) * step, :], right,
                preferred_element_type=jnp.float32,
            )
            for q in range(step // sub):
                for h in range(halves):
                    cut = block[q * sub : (q + 1) * sub, h * LANES : (h + 1) * LANES]
                    stats[h] = join(*stats[h], cut)
        for tile, (peak, total) in zip(tiles, stats):
            if lse_ref is None:
                stats_ref[0, tile] = peak
                stats_ref[1, tile] = total
            else:
                top, total = closed(peak, total)
                lse_ref[pl.ds(tile, 1), :] = top + jnp.log2(total)
        return unused

    lax.fori_loop(0, (end - begin) // width, over_columns, 0, unroll=True)


def fill_tile(rows_ref, right, tile_ref, row_span, peak):
    low, high = row_span
    width = tile_ref.shape[1]
    step = math.gcd(high - low, STEP)
    for r in range((high - low) // step):
        at = slice(low + r * step, low + (r + 1) * step)
        block = jnp.dot(rows_ref[at, :], right, preferred_element_type=jnp.float32)
        tile_ref[at, :] = block
        peak = jnp.maximum(peak, jnp.max(block.reshape(-1, 8, width), axis=0))
    return peak


def carry_tile(tile_ref, peak, scores_ref, weights):
    rows = tile_ref.shape[0]
    step = math.gcd(rows, STEP)
    for r in range(rows // step):
        at = slice(r * step, (r + 1) * step)
        weights[at, :] = jnp.exp2(tile_ref[at, :] - peak).astype(jnp.bfloat16)
    return jnp.dot(scores_ref[...], weights[...], preferred_element_type=jnp.float32)


def kernel(
    n_src, n_tgt, xs_ref, yt_ref, growth_ref, scores_ref, f_ref, g_ref, out_ref,
    tile, x_wide, y_wide, x_rows, x_cols, y_rows, y_cols, scores_t, weights, running, sums, peaks, pay,
    row_buf, col_buf, f_all, row_send, row_recv, col_send, col_recv,
    bulk_send, bulk_recv, pass_send, pass_recv, f_send, f_recv,
):
    src, tgt = lax.axis_index("src"), lax.axis_index("tgt")
    barrier = pltpu.get_barrier_semaphore()
    for k in range(1, n_src):
        pl.semaphore_signal(
            barrier, inc=1, device_id={"src": lax.rem(src + k, n_src)}, device_id_type=MESH
        )
    for k in range(1, n_tgt):
        pl.semaphore_signal(
            barrier, inc=1, device_id={"tgt": lax.rem(tgt + k, n_tgt)}, device_id_type=MESH
        )

    pcs, rows = xs_ref.shape
    columns = yt_ref.shape[1]
    programs = scores_ref.shape[1]
    scale = 2.0 * LOG2E / (pcs * EPSILON)
    bias_at = 3 * depth_of(pcs)[0] + 8
    augment(yt_ref[...], y_wide, scale, False)
    y_cols[...] = y_wide[...].astype(jnp.bfloat16)
    turn(y_wide, y_rows, 0, columns)
    augment(xs_ref[...], x_wide.at[0], scale, True)
    x_cols[...] = x_wide[0].astype(jnp.bfloat16)

    pay[0, programs:, :] = jnp.zeros((pay.shape[1] - programs, rows), jnp.float32)
    pay[0, programs : programs + pcs, :] = xs_ref[...].astype(jnp.float32)
    for k in range(rows // LANES):
        cut = slice(k * LANES, (k + 1) * LANES)
        pay[0, 0:programs, cut] = scores_ref[cut, :].astype(jnp.float32).T
    scores_t[0, 0:programs, :] = pay[0, 0:programs, :].astype(jnp.bfloat16)
    for p in range(2):
        scores_t[p, programs:, :] = jnp.ones((16, rows), jnp.bfloat16)

    bits = [1 << b for b in range(n_src.bit_length() - 1)]
    core, share = lax.rem(tgt, 2), pay.shape[1] // 4

    def relative(mask):
        there = src
        for bit in bits:
            if mask & bit:
                there = there + bit - 2 * bit * lax.rem(lax.div(src, bit), 2)
        return there

    def lines_at(order):
        return pl.ds(pl.multiple_of((2 * core + order) * share, 8), share)

    bulk, passed = {}, {}

    def ship(order, bit, mask):
        lines = lines_at(order)
        copy = pltpu.make_async_remote_copy(
            src_ref=pay.at[mask, lines], dst_ref=pay.at[mask ^ bit, lines],
            send_sem=bulk_send.at[order, mask ^ bit], recv_sem=bulk_recv.at[order, mask ^ bit],
            device_id={"src": relative(bit)}, device_id_type=MESH,
        )
        copy.start()
        bulk[order, mask ^ bit] = copy

    def hand_over(order, mask):
        if (order, mask) in passed:
            return
        bulk[order, mask].wait_recv()
        lines = lines_at(order)
        copy = pltpu.make_async_remote_copy(
            src_ref=pay.at[mask, lines], dst_ref=pay.at[mask, lines],
            send_sem=pass_send.at[order, mask], recv_sem=pass_recv.at[order, mask],
            device_id={"tgt": tgt + 1 - 2 * core}, device_id_type=MESH,
        )
        copy.start()
        passed[order, mask] = copy

    orders = [bits, bits[::-1]]

    def ship_first():
        for order, bit in enumerate(orders):
            ship(order, bit[0], 0)

    def ship_own():
        for order, bit in enumerate(orders):
            for b in bit[1:]:
                ship(order, b, 0)
            hand_over(order, bit[0])

    def ship_rest():
        for t in range(1, len(bits)):
            for order, bit in enumerate(orders):
                held = [0]
                for b in bit[:t]:
                    held += [m ^ b for m in held]
                for mask in held[1:]:
                    hand_over(order, mask)
                    ship(order, bit[t], mask)

    def exchange(buf, axis, me, n, send, recv, lines):
        copies = [
            pltpu.make_async_remote_copy(
                src_ref=buf.at[me, lines], dst_ref=buf.at[me, lines],
                send_sem=send.at[k], recv_sem=recv.at[k],
                device_id={axis: lax.rem(me + k, n)}, device_id_type=MESH,
            )
            for k in range(1, n)
        ]
        for copy in copies:
            copy.start()
        return copies

    def joined(buf, n, lines):
        parts = [buf[d, lines] for d in range(n)]
        top = functools.reduce(jnp.maximum, parts)
        return top + jnp.log2(sum(jnp.exp2(part - top) for part in parts))

    log_a = jnp.log2(growth_ref[...]) - math.log2(rows * n_src)
    log_b = -math.log2(columns * n_tgt)
    source_halves, target_halves = halves_of(rows), halves_of(columns)

    def lines_of(span):
        return slice(span[0] // LANES, span[1] // LANES)

    def finish(rows_ref, columns_ref, row_span, spans, fresh, buf, axis, me, n, send, recv):
        sent = []
        for h, span in enumerate(spans):
            lse_pass(rows_ref, columns_ref, running, buf.at[me], row_span, span, fresh)
            sent.append(exchange(buf, axis, me, n, send.at[h], recv.at[h], lines_of(span)))
        return sent

    def settle(copies):
        for copy in copies:
            copy.wait()

    for step in range(ITERS):
        over_tgt = (row_buf.at[step], "tgt", tgt, n_tgt, row_send.at[step], row_recv.at[step])
        over_src = (col_buf.at[step], "src", src, n_src, col_send.at[step], col_recv.at[step])
        if step == 0:
            pl.semaphore_wait(barrier, n_src + n_tgt - 2)
            ship_first()
            sent = finish(y_rows, x_cols, (0, columns), source_halves, True, *over_tgt)
        else:
            for h, span in enumerate(target_halves):
                settle(sent[h])
                lines = lines_of(span)
                g = FACTOR * (log_b - joined(col_buf.at[step - 1], n_src, lines))
                set_bias(g, y_wide, y_rows, bias_at + 3, span[0])
                if h < len(target_halves) - 1:
                    lse_pass(y_rows, x_cols, running, None, span, (0, rows), h == 0)
            sent = finish(y_rows, x_cols, span, source_halves, h == 0, *over_tgt)
        if step == ITERS - 1:
            break
        for h, span in enumerate(source_halves):
            settle(sent[h])
            lines = lines_of(span)
            f = FACTOR * (log_a[lines] - joined(row_buf.at[step], n_tgt, lines))
            set_bias(f, x_wide.at[0], x_rows.at[0], bias_at, span[0])
            if h < len(source_halves) - 1:
                lse_pass(x_rows.at[0], y_cols, running, None, span, (0, columns), h == 0)
        sent = finish(x_rows.at[0], y_cols, span, target_halves, h == 0, *over_src)
        if step == 0:
            ship_own()

    width = math.gcd(columns, WIDTH)
    groups, halves = columns // width, width // LANES
    empty = jnp.full((8, width), -jnp.inf, jnp.float32)

    def lanes_of(c):
        return pl.ds(pl.multiple_of(c * width, width), width)

    def fill(block, c, slot, span, peak):
        return fill_tile(x_rows.at[block % 2], y_cols[:, lanes_of(c)], tile.at[slot], span, peak)

    def prepare(block):
        for order in range(2):
            hand_over(order, block)
        for order in range(2):
            passed[order, block].wait_recv()
        shared[block].wait_recv()
        slot = block % 2
        wide_ref, rows_ref = x_wide.at[slot], x_rows.at[slot]
        augment(pay[block, programs : programs + pcs, :], wide_ref, scale, True)
        set_bias(f_all[block], wide_ref, rows_ref, bias_at, 0)
        scores_t[slot, 0:programs, :] = pay[block, 0:programs, :].astype(jnp.bfloat16)

    def carry(block, c, slot, ready):
        lanes = lanes_of(c)
        peak = jnp.max(ready, axis=0, keepdims=True)
        if block > 0:
            before = peaks[0:1, lanes]
            peak = jnp.maximum(peak, before)
        carried = carry_tile(tile.at[slot], peak, scores_t.at[block % 2], weights.at[slot])
        if block > 0:
            carried = carried + sums[:, lanes] * jnp.exp2(before - peak)
        if block < n_src - 1:
            sums[:, lanes] = carried
            peaks[0:1, lanes] = peak
            return
        mass = carried[programs : programs + 1, :]
        g = UNIT * FACTOR * (log_b - (peak + jnp.log2(mass)))
        carried = carried[0:programs, :] / mass
        for h in range(halves):
            cut = slice(h * LANES, (h + 1) * LANES)
            g_ref[pl.ds(c * halves + h, 1), :] = g[:, cut]
            at = pl.ds(pl.multiple_of(c * width + h * LANES, LANES), LANES)
            out_ref[at, :] = carried[:, cut].T

    ready = empty
    for h, span in enumerate(source_halves):
        settle(sent[h])
        lines = lines_of(span)
        f = FACTOR * (log_a[lines] - joined(row_buf.at[ITERS - 1], n_tgt, lines))
        f_ref[lines, :] = UNIT * f
        f_all[0, lines, :] = f
        if h == len(source_halves) - 1:
            shared = {}
            for mask in range(1, n_src):
                shared[mask] = pltpu.make_async_remote_copy(
                    src_ref=f_all.at[0], dst_ref=f_all.at[mask],
                    send_sem=f_send.at[mask], recv_sem=f_recv.at[mask],
                    device_id={"src": relative(mask)}, device_id_type=MESH,
                )
                shared[mask].start()
            ship_rest()
        set_bias(f, x_wide.at[0], x_rows.at[0], bias_at, span[0])
        if n_src <= 4:
            ready = fill(0, 0, 0, span, ready)
    if n_src <= 4:
        units = [(block, c) for block in range(n_src) for c in range(groups)]
        for u, (block, c) in enumerate(units):
            now = ready
            if c == 0 and groups > 1 and block + 1 < n_src:
                for order in range(2):
                    hand_over(order, block + 1)
            if c == groups // 2 and block + 1 < n_src:
                prepare(block + 1)
            if u + 1 < len(units):
                ready = fill(*units[u + 1], (u + 1) % 2, (0, rows), empty)
            carry(block, c, u % 2, now)
    else:
        for block in range(n_src):
            if block > 0:
                prepare(block)

            def over_groups(c, unused, block=block):
                carry(block, c, 0, fill(block, c, 0, (0, rows), empty))
                return unused

            lax.fori_loop(0, groups, over_groups, 0)
    for copy in [*bulk.values(), *passed.values(), *shared.values()]:
        copy.wait_send()


def solution(mesh):
    n_src, n_tgt = mesh.shape["src"], mesh.shape["tgt"]

    def shards(pcs_source, pcs_target, growth, scores):
        rows, columns = pcs_source.shape[1], pcs_target.shape[1]
        programs = scores.shape[1]
        width = math.gcd(columns, WIDTH)
        pcs = pcs_source.shape[0]
        depth = depth_of(pcs)[1]
        f32, bf16 = jnp.float32, jnp.bfloat16
        sem = pltpu.SemaphoreType.DMA
        whole = pl.BlockSpec(memory_space=pltpu.VMEM)
        dense_r, dense_c = (rows // LANES, LANES), (columns // LANES, LANES)
        f, g, out = pl.pallas_call(
            functools.partial(kernel, n_src, n_tgt),
            out_shape=(
                jax.ShapeDtypeStruct(dense_r, f32),
                jax.ShapeDtypeStruct(dense_c, f32),
                jax.ShapeDtypeStruct((columns, programs), f32),
            ),
            in_specs=[whole] * 4,
            out_specs=(whole,) * 3,
            scratch_shapes=[
                pltpu.VMEM((2, rows, width), f32),
                pltpu.VMEM((2, depth, rows), f32),
                pltpu.VMEM((depth, columns), f32),
                pltpu.VMEM((2, rows, depth), bf16),
                pltpu.VMEM((depth, rows), bf16),
                pltpu.VMEM((columns, depth), bf16),
                pltpu.VMEM((depth, columns), bf16),
                pltpu.VMEM((2, programs + 16, rows), bf16),
                pltpu.VMEM((2, rows, width), bf16),
                pltpu.VMEM((2, max(rows, columns) // LANES, 8, LANES), f32),
                pltpu.VMEM((programs + 16, columns), f32),
                pltpu.VMEM((8, columns), f32),
                pltpu.VMEM((n_src, -(-(programs + pcs) // 32) * 32, rows), f32),
                pltpu.VMEM((ITERS, n_tgt) + dense_r, f32),
                pltpu.VMEM((ITERS, n_src) + dense_c, f32),
                pltpu.VMEM((n_src,) + dense_r, f32),
                sem((ITERS, 2, n_tgt)),
                sem((ITERS, 2, n_tgt)),
                sem((ITERS, 2, n_src)),
                sem((ITERS, 2, n_src)),
                sem((2, n_src)),
                sem((2, n_src)),
                sem((2, n_src)),
                sem((2, n_src)),
                sem((n_src,)),
                sem((n_src,)),
            ],
            compiler_params=pltpu.CompilerParams(
                collective_id=0, has_side_effects=True, vmem_limit_bytes=60 * 2**20
            ),
            name="coupling",
        )(pcs_source, pcs_target, growth.reshape(dense_r), scores)
        return f.reshape(-1), g.reshape(-1), out

    in_specs = (P(None, "src"), P(None, "tgt"), P("src"), P("src", None))
    out_specs = (P("src"), P("tgt"), P("tgt", None))
    return jax.shard_map(shards, mesh=mesh, in_specs=in_specs, out_specs=out_specs, check_vma=False)
```

```python
import functools
import math

import jax
import jax.numpy as jnp
from jax import lax
from jax.experimental import pallas as pl
from jax.experimental.pallas import tpu as pltpu
from jax.sharding import PartitionSpec as P

ITERS = 2
EPSILON = 0.05
MARGIN = 1.0
FACTOR = MARGIN / (MARGIN + EPSILON)
LANES = 128
LOG2E = math.log2(math.e)
UNIT = EPSILON / LOG2E
MESH = pl.DeviceIdType.MESH
WIDTH, STEP, SUB = 512, 256, 64


def split3(value):
    high = value.astype(jnp.bfloat16).astype(jnp.float32)
    mid = (value - high).astype(jnp.bfloat16).astype(jnp.float32)
    return high, mid, value - high - mid


def depth_of(pcs):
    base = -(-pcs // 8) * 8
    return base, -(-(3 * base + 16) // LANES) * LANES


def augment(coords, wide_ref, scale, source):
    pcs, cells = coords.shape
    base, depth = depth_of(pcs)
    wide = coords.astype(jnp.float32)
    norm = -0.5 * scale * jnp.sum(wide * wide, axis=0, keepdims=True)
    at = lax.broadcasted_iota(jnp.int32, (16, cells), 0) - (0 if source else 3)
    high, mid, low = split3(norm)
    extra = jnp.where(at == 0, high, jnp.where(at == 1, mid, jnp.where(at == 2, low, 0.0)))
    at = lax.broadcasted_iota(jnp.int32, (16, cells), 0)
    ones = ((at >= 3) & (at < 6)) | ((at >= 11) & (at < 14)) if source else (at < 3) | ((at >= 8) & (at < 11))
    wide_ref[...] = jnp.zeros(wide_ref.shape, jnp.float32)
    for k, piece in enumerate(split3(scale * wide) if source else (wide,) * 3):
        wide_ref[k * base : k * base + pcs, :] = piece
    wide_ref[3 * base : 3 * base + 16, :] = jnp.where(ones, 1.0, extra)


def turn(wide_ref, rows_ref, first, last):
    depth = wide_ref.shape[0]
    for k in range(first // LANES, last // LANES):
        cut = slice(k * LANES, (k + 1) * LANES)
        for d in range(depth // LANES):
            deep = slice(d * LANES, (d + 1) * LANES)
            rows_ref[cut, deep] = wide_ref[deep, cut].T.astype(jnp.bfloat16)


def set_bias(dense, wide_ref, rows_ref, at, first):
    cells = dense.shape[0] * LANES
    for p, piece in enumerate(split3(dense)):
        for k in range(dense.shape[0]):
            lanes = slice(first + k * LANES, first + (k + 1) * LANES)
            wide_ref[at + p : at + p + 1, lanes] = piece[k : k + 1, :]
    turn(wide_ref, rows_ref, first, first + cells)


def halves_of(cells):
    parts = math.gcd(2, max(cells // (8 * LANES), 1))
    return [(p * (cells // parts), (p + 1) * (cells // parts)) for p in range(parts)]


def join(peak, total, block):
    t = block.reshape(-1, 8, LANES)
    newpeak = jnp.maximum(peak, jnp.max(t, axis=0))
    total = total * jnp.exp2(peak - newpeak) + jnp.sum(jnp.exp2(t - newpeak[None]), axis=0)
    return newpeak, total


def closed(peak, total):
    top = jnp.max(peak, axis=0, keepdims=True)
    return top, jnp.sum(total * jnp.exp2(peak - top), axis=0, keepdims=True)


def lse_pass(rows_ref, columns_ref, stats_ref, lse_ref, row_span, lane_span, fresh):
    (low, high), (begin, end) = row_span, lane_span
    width = math.gcd(end - begin, WIDTH)
    step = math.gcd(high - low, STEP)
    sub = math.gcd(step, SUB)
    halves = width // LANES

    def over_columns(c, unused):
        right = columns_ref[:, pl.ds(pl.multiple_of(begin + c * width, width), width)]
        tiles = [begin // LANES + c * halves + h for h in range(halves)]
        if fresh:
            empty = (jnp.full((8, LANES), -jnp.inf, jnp.float32), jnp.zeros((8, LANES), jnp.float32))
            stats = [empty] * halves
        else:
            stats = [(stats_ref[0, tile], stats_ref[1, tile]) for tile in tiles]
        for r in range((high - low) // step):
            block = jnp.dot(
                rows_ref[low + r * step : low + (r + 1) * step, :], right,
                preferred_element_type=jnp.float32,
            )
            for q in range(step // sub):
                for h in range(halves):
                    cut = block[q * sub : (q + 1) * sub, h * LANES : (h + 1) * LANES]
                    stats[h] = join(*stats[h], cut)
        for tile, (peak, total) in zip(tiles, stats):
            if lse_ref is None:
                stats_ref[0, tile] = peak
                stats_ref[1, tile] = total
            else:
                top, total = closed(peak, total)
                lse_ref[pl.ds(tile, 1), :] = top + jnp.log2(total)
        return unused

    lax.fori_loop(0, (end - begin) // width, over_columns, 0, unroll=True)


def fill_tile(rows_ref, right, tile_ref, row_span, peak):
    low, high = row_span
    width = tile_ref.shape[1]
    step = math.gcd(high - low, STEP)
    for r in range((high - low) // step):
        at = slice(low + r * step, low + (r + 1) * step)
        block = jnp.dot(rows_ref[at, :], right, preferred_element_type=jnp.float32)
        tile_ref[at, :] = block
        peak = jnp.maximum(peak, jnp.max(block.reshape(-1, 8, width), axis=0))
    return peak


def carry_tile(tile_ref, peak, scores_ref, weights):
    rows = tile_ref.shape[0]
    step = math.gcd(rows, STEP)
    for r in range(rows // step):
        at = slice(r * step, (r + 1) * step)
        weights[at, :] = jnp.exp2(tile_ref[at, :] - peak).astype(jnp.bfloat16)
    return jnp.dot(scores_ref[...], weights[...], preferred_element_type=jnp.float32)


def kernel(
    n_src, n_tgt, xs_ref, yt_ref, growth_ref, scores_ref, f_ref, g_ref, out_ref,
    tile, x_wide, y_wide, x_rows, x_cols, y_rows, y_cols, scores_t, weights, running, sums, peaks, pay,
    row_buf, col_buf, f_all, g_all, row_send, row_recv, col_send, col_recv,
    bulk_send, bulk_recv, pass_send, pass_recv, f_send, f_recv, out_send, out_recv,
):
    src, tgt = lax.axis_index("src"), lax.axis_index("tgt")
    barrier = pltpu.get_barrier_semaphore()
    for k in range(1, n_src):
        pl.semaphore_signal(
            barrier, inc=1, device_id={"src": lax.rem(src + k, n_src)}, device_id_type=MESH
        )
    for k in range(1, n_tgt):
        pl.semaphore_signal(
            barrier, inc=1, device_id={"tgt": lax.rem(tgt + k, n_tgt)}, device_id_type=MESH
        )

    pcs, rows = xs_ref.shape
    columns = yt_ref.shape[1]
    programs = scores_ref.shape[1]
    scale = 2.0 * LOG2E / (pcs * EPSILON)
    bias_at = 3 * depth_of(pcs)[0] + 8
    augment(yt_ref[...], y_wide, scale, False)
    y_cols[...] = y_wide[...].astype(jnp.bfloat16)
    turn(y_wide, y_rows, 0, columns)
    augment(xs_ref[...], x_wide.at[0], scale, True)
    x_cols[...] = x_wide[0].astype(jnp.bfloat16)

    pay[0, programs:, :] = jnp.zeros((pay.shape[1] - programs, rows), jnp.float32)
    pay[0, programs : programs + pcs, :] = xs_ref[...].astype(jnp.float32)
    for k in range(rows // LANES):
        cut = slice(k * LANES, (k + 1) * LANES)
        pay[0, 0:programs, cut] = scores_ref[cut, :].astype(jnp.float32).T
    scores_t[0, 0:programs, :] = pay[0, 0:programs, :].astype(jnp.bfloat16)
    for p in range(scores_t.shape[0]):
        scores_t[p, programs:, :] = jnp.ones((16, rows), jnp.bfloat16)

    bits = [1 << b for b in range(n_src.bit_length() - 1)]
    core, share = lax.rem(tgt, 2), pay.shape[1] // 4

    def relative(mask):
        there = src
        for bit in bits:
            if mask & bit:
                there = there + bit - 2 * bit * lax.rem(lax.div(src, bit), 2)
        return there

    early = share // 3 // 8 * 8
    spans_of_share = [(0, early), (early, share)] if early else [(0, share)]
    parts = range(len(spans_of_share))

    def lines_at(order, part):
        low, high = spans_of_share[part]
        return pl.ds(pl.multiple_of((2 * core + order) * share + low, 8), high - low)

    bulk, passed = {}, {}

    def ship(order, bit, mask, part):
        lines, there = lines_at(order, part), mask ^ bit
        copy = pltpu.make_async_remote_copy(
            src_ref=pay.at[mask, lines], dst_ref=pay.at[there, lines],
            send_sem=bulk_send.at[order, there, part], recv_sem=bulk_recv.at[order, there, part],
            device_id={"src": relative(bit)}, device_id_type=MESH,
        )
        copy.start()
        bulk[order, there, part] = copy

    def hand_over(mask, chosen=(0, 1)):
        for part in parts:
            for order in chosen:
                if (order, mask, part) in passed:
                    continue
                bulk[order, mask, part].wait_recv()
                lines = lines_at(order, part)
                copy = pltpu.make_async_remote_copy(
                    src_ref=pay.at[mask, lines], dst_ref=pay.at[mask, lines],
                    send_sem=pass_send.at[order, mask, part],
                    recv_sem=pass_recv.at[order, mask, part],
                    device_id={"tgt": tgt + 1 - 2 * core}, device_id_type=MESH,
                )
                copy.start()
                passed[order, mask, part] = copy

    orders = [bits, bits[::-1]]

    def ship_own(stages, chosen):
        for t in stages:
            for part in chosen:
                for order, bit in enumerate(orders):
                    ship(order, bit[t], 0, part)

    def ship_rest():
        for order, bit in enumerate(orders):
            hand_over(bit[0], (order,))
        for t in range(1, len(bits)):
            for order, bit in enumerate(orders):
                held = [0]
                for b in bit[:t]:
                    held += [m ^ b for m in held]
                for mask in held[1:]:
                    hand_over(mask, (order,))
                    for part in parts:
                        ship(order, bit[t], mask, part)

    def exchange(buf, axis, me, n, send, recv, lines):
        copies = [
            pltpu.make_async_remote_copy(
                src_ref=buf.at[me, lines], dst_ref=buf.at[me, lines],
                send_sem=send.at[k], recv_sem=recv.at[k],
                device_id={axis: lax.rem(me + k, n)}, device_id_type=MESH,
            )
            for k in range(1, n)
        ]
        for copy in copies:
            copy.start()
        return copies

    def joined(buf, n, lines):
        parts = [buf[d, lines] for d in range(n)]
        top = functools.reduce(jnp.maximum, parts)
        return top + jnp.log2(sum(jnp.exp2(part - top) for part in parts))

    log_a = jnp.log2(growth_ref[...]) - math.log2(rows * n_src)
    log_b = -math.log2(columns * n_tgt)
    quarters = n_src == 4
    source_halves, target_halves = halves_of(rows), halves_of(columns)

    def lines_of(span):
        return slice(span[0] // LANES, span[1] // LANES)

    def finish(rows_ref, columns_ref, row_span, spans, fresh, buf, axis, me, n, send, recv):
        sent = []
        for h, span in enumerate(spans):
            lse_pass(rows_ref, columns_ref, running, buf.at[me], row_span, span, fresh)
            sent.append(exchange(buf, axis, me, n, send.at[h], recv.at[h], lines_of(span)))
        return sent

    def settle(copies):
        for copy in copies:
            copy.wait()

    for step in range(ITERS):
        over_tgt = (row_buf.at[step], "tgt", tgt, n_tgt, row_send.at[step], row_recv.at[step])
        over_src = (col_buf.at[step], "src", src, n_src, col_send.at[step], col_recv.at[step])
        if step == 0:
            pl.semaphore_wait(barrier, n_src + n_tgt - 2)
            ship_own(range(1), parts)
            ship_own(range(1, len(bits)), parts[:1])
            sent = finish(y_rows, x_cols, (0, columns), source_halves, True, *over_tgt)
        else:
            for h, span in enumerate(target_halves):
                settle(sent[h])
                lines = lines_of(span)
                g = FACTOR * (log_b - joined(col_buf.at[step - 1], n_src, lines))
                set_bias(g, y_wide, y_rows, bias_at + 3, span[0])
                if h < len(target_halves) - 1:
                    lse_pass(y_rows, x_cols, running, None, span, (0, rows), h == 0)
            sent = finish(y_rows, x_cols, span, source_halves, h == 0, *over_tgt)
        if step == ITERS - 1:
            break
        for h, span in enumerate(source_halves):
            settle(sent[h])
            lines = lines_of(span)
            f = FACTOR * (log_a[lines] - joined(row_buf.at[step], n_tgt, lines))
            set_bias(f, x_wide.at[0], x_rows.at[0], bias_at, span[0])
            if h < len(source_halves) - 1:
                lse_pass(x_rows.at[0], y_cols, running, None, span, (0, columns), h == 0)
        sent = finish(x_rows.at[0], y_cols, span, target_halves, h == 0, *over_src)
        if step == 0:
            ship_own(range(1, len(bits)), parts[1:])
            if quarters:
                ship_rest()

    width, slots = tile.shape[2], x_rows.shape[0]
    groups, halves = columns // width, width // LANES
    piece = columns // n_src
    empty = jnp.full((8, width), -jnp.inf, jnp.float32)

    def fill(block, start, slot, span, peak):
        right = y_cols[:, pl.ds(pl.multiple_of(start, width), width)]
        return fill_tile(x_rows.at[block % slots], right, tile.at[slot], span, peak)

    def unpack(block):
        hand_over(block)
        for order in range(2):
            for part in parts:
                passed[order, block, part].wait_recv()
        augment(pay[block, programs : programs + pcs, :], x_wide.at[block % slots], scale, True)
        scores_t[block % slots, 0:programs, :] = pay[block, 0:programs, :].astype(jnp.bfloat16)

    def admit(block):
        shared[block].wait_recv()
        slot = block % slots
        set_bias(f_all[block], x_wide.at[slot], x_rows.at[slot], bias_at, 0)

    def carry(block, start, place, slot, ready):
        peak = jnp.max(ready, axis=0, keepdims=True)
        if block > 0:
            before = peaks[place, 0:1, :]
            peak = jnp.maximum(peak, before)
        carried = carry_tile(tile.at[slot], peak, scores_t.at[block % slots], weights.at[slot])
        if block > 0:
            carried = carried + sums[place] * jnp.exp2(before - peak)
        if block < n_src - 1:
            sums[place] = carried
            peaks[place, 0:1, :] = peak
            return
        mass = carried[programs : programs + 1, :]
        g = UNIT * FACTOR * (log_b - (peak + jnp.log2(mass)))
        carried = carried[0:programs, :] / mass
        for h in range(halves):
            cut = slice(h * LANES, (h + 1) * LANES)
            at = start + h * LANES
            owner = lax.div(at, piece)
            g_all[owner, pl.ds(lax.div(at - owner * piece, LANES), 1), :] = g[:, cut]
            out_ref[pl.ds(pl.multiple_of(at, LANES), LANES), :] = carried[:, cut].T

    for block in range(1, n_src):
        if quarters and block < n_src - 1:
            hand_over(block)
    ready, shared = empty, {}
    for h, span in enumerate(source_halves):
        settle(sent[h])
        lines = lines_of(span)
        f = FACTOR * (log_a[lines] - joined(row_buf.at[ITERS - 1], n_tgt, lines))
        f_ref[lines, :] = UNIT * f
        f_all[0, lines, :] = f
        if h == len(source_halves) - 1:
            for mask in range(1, n_src):
                shared[mask] = pltpu.make_async_remote_copy(
                    src_ref=f_all.at[0], dst_ref=f_all.at[mask],
                    send_sem=f_send.at[mask], recv_sem=f_recv.at[mask],
                    device_id={"src": relative(mask)}, device_id_type=MESH,
                )
                shared[mask].start()
            if not quarters:
                ship_rest()
        set_bias(f, x_wide.at[0], x_rows.at[0], bias_at, span[0])
        if quarters:
            ready = fill(0, src * piece, 0, span, ready)

    gathered = []
    if quarters:
        wide = piece // width
        mine = [(src * piece + c * width, c) for c in range(wide)]
        spare = [((3 - src) * piece + c * width, wide + c) for c in range(wide)]
        order = [(0, spot) for spot in mine + spare]
        order += [(block, spot) for block in range(1, n_src) for spot in mine]
        order += [(block, spot) for block in range(1, n_src) for spot in spare]
        for u, (block, spot) in enumerate(order):
            now, after = ready, order[u + 1] if u + 1 < len(order) else None
            fresh = after and after[0] > block and u < 2 * wide + (n_src - 1) * wide - 1
            if fresh and after[0] == 1:
                carry(block, *spot, u % 2, now)
                now = None
                hand_over(n_src - 1)
            if fresh:
                unpack(after[0])
                admit(after[0])
            if after:
                ready = fill(after[0], after[1][0], (u + 1) % 2, (0, rows), empty)
            if now is not None:
                carry(block, *spot, u % 2, now)
            if u == 2 * wide + (n_src - 1) * wide - 1:
                at = pl.ds(pl.multiple_of(src * piece, piece), piece)
                for k, bit in enumerate(bits):
                    for slot, ref in enumerate((out_ref.at[at, :], g_all.at[src])):
                        copy = pltpu.make_async_remote_copy(
                            src_ref=ref, dst_ref=ref,
                            send_sem=out_send.at[slot, k], recv_sem=out_recv.at[slot, k],
                            device_id={"src": relative(bit)}, device_id_type=MESH,
                        )
                        copy.start()
                        gathered.append(copy)
    else:
        for block in range(n_src):
            if block > 0:
                unpack(block)
                admit(block)

            def over_groups(c, unused, block=block):
                start = c * width
                carry(block, start, c, 0, fill(block, start, 0, (0, rows), empty))
                return unused

            lax.fori_loop(0, groups, over_groups, 0)
    for copy in gathered:
        copy.wait()
    for k in range(n_src):
        g_ref[k * (piece // LANES) : (k + 1) * (piece // LANES), :] = g_all[k, 0 : piece // LANES, :]
    for copy in [*bulk.values(), *passed.values(), *shared.values()]:
        copy.wait_send()


def solution(mesh):
    n_src, n_tgt = mesh.shape["src"], mesh.shape["tgt"]

    def shards(pcs_source, pcs_target, growth, scores):
        rows, columns = pcs_source.shape[1], pcs_target.shape[1]
        programs = scores.shape[1]
        width, slots = math.gcd(columns, WIDTH), 2
        if n_src == 4:
            width, slots = math.gcd(columns // n_src, WIDTH), n_src
        pcs = pcs_source.shape[0]
        depth = depth_of(pcs)[1]
        f32, bf16 = jnp.float32, jnp.bfloat16
        sem = pltpu.SemaphoreType.DMA
        whole = pl.BlockSpec(memory_space=pltpu.VMEM)
        dense_r, dense_c = (rows // LANES, LANES), (columns // LANES, LANES)
        f, g, out = pl.pallas_call(
            functools.partial(kernel, n_src, n_tgt),
            out_shape=(
                jax.ShapeDtypeStruct(dense_r, f32),
                jax.ShapeDtypeStruct(dense_c, f32),
                jax.ShapeDtypeStruct((columns, programs), f32),
            ),
            in_specs=[whole] * 4,
            out_specs=(whole,) * 3,
            scratch_shapes=[
                pltpu.VMEM((2, rows, width), f32),
                pltpu.VMEM((slots, depth, rows), f32),
                pltpu.VMEM((depth, columns), f32),
                pltpu.VMEM((slots, rows, depth), bf16),
                pltpu.VMEM((depth, rows), bf16),
                pltpu.VMEM((columns, depth), bf16),
                pltpu.VMEM((depth, columns), bf16),
                pltpu.VMEM((slots, programs + 16, rows), bf16),
                pltpu.VMEM((2, rows, width), bf16),
                pltpu.VMEM((2, max(rows, columns) // LANES, 8, LANES), f32),
                pltpu.VMEM((columns // width, programs + 16, width), f32),
                pltpu.VMEM((columns // width, 8, width), f32),
                pltpu.VMEM((n_src, -(-(programs + pcs) // 32) * 32, rows), f32),
                pltpu.VMEM((ITERS, n_tgt) + dense_r, f32),
                pltpu.VMEM((ITERS, n_src) + dense_c, f32),
                pltpu.VMEM((n_src,) + dense_r, f32),
                pltpu.VMEM((n_src, -(-columns // n_src // (8 * LANES)) * 8, LANES), f32),
                sem((ITERS, 2, n_tgt)),
                sem((ITERS, 2, n_tgt)),
                sem((ITERS, 2, n_src)),
                sem((ITERS, 2, n_src)),
                sem((2, n_src, 2)),
                sem((2, n_src, 2)),
                sem((2, n_src, 2)),
                sem((2, n_src, 2)),
                sem((n_src,)),
                sem((n_src,)),
                sem((2, 2)),
                sem((2, 2)),
            ],
            compiler_params=pltpu.CompilerParams(
                collective_id=0, has_side_effects=True, vmem_limit_bytes=60 * 2**20
            ),
            name="coupling",
        )(pcs_source, pcs_target, growth.reshape(dense_r), scores)
        return f.reshape(-1), g.reshape(-1), out

    in_specs = (P(None, "src"), P(None, "tgt"), P("src"), P("src", None))
    out_specs = (P("src"), P("tgt"), P("tgt", None))
    return jax.shard_map(shards, mesh=mesh, in_specs=in_specs, out_specs=out_specs, check_vma=False)
```

```python
import functools
import math

import jax
import jax.numpy as jnp
from jax import lax
from jax.experimental import pallas as pl
from jax.experimental.pallas import tpu as pltpu
from jax.sharding import PartitionSpec as P

ITERS = 2
EPSILON = 0.05
MARGIN = 1.0
FACTOR = MARGIN / (MARGIN + EPSILON)
LANES = 128
LOG2E = math.log2(math.e)
UNIT = EPSILON / LOG2E
MESH = pl.DeviceIdType.MESH
WIDTH, STEP, SUB = 512, 256, 64


def split3(value):
    high = value.astype(jnp.bfloat16).astype(jnp.float32)
    mid = (value - high).astype(jnp.bfloat16).astype(jnp.float32)
    return high, mid, value - high - mid


def depth_of(pcs):
    base = -(-pcs // 8) * 8
    return base, -(-(3 * base + 16) // LANES) * LANES


def augment(coords, wide_ref, scale, source):
    pcs, cells = coords.shape
    base, depth = depth_of(pcs)
    wide = coords.astype(jnp.float32)
    norm = -0.5 * scale * jnp.sum(wide * wide, axis=0, keepdims=True)
    at = lax.broadcasted_iota(jnp.int32, (16, cells), 0) - (0 if source else 3)
    high, mid, low = split3(norm)
    extra = jnp.where(at == 0, high, jnp.where(at == 1, mid, jnp.where(at == 2, low, 0.0)))
    at = lax.broadcasted_iota(jnp.int32, (16, cells), 0)
    ones = ((at >= 3) & (at < 6)) | ((at >= 11) & (at < 14)) if source else (at < 3) | ((at >= 8) & (at < 11))
    wide_ref[...] = jnp.zeros(wide_ref.shape, jnp.float32)
    for k, piece in enumerate(split3(scale * wide) if source else (wide,) * 3):
        wide_ref[k * base : k * base + pcs, :] = piece
    wide_ref[3 * base : 3 * base + 16, :] = jnp.where(ones, 1.0, extra)


def turn(wide_ref, rows_ref, first, last):
    depth = wide_ref.shape[0]
    for k in range(first // LANES, last // LANES):
        cut = slice(k * LANES, (k + 1) * LANES)
        for d in range(depth // LANES):
            deep = slice(d * LANES, (d + 1) * LANES)
            rows_ref[cut, deep] = wide_ref[deep, cut].T.astype(jnp.bfloat16)


def set_bias(dense, wide_ref, rows_ref, at, first):
    cells = dense.shape[0] * LANES
    for p, piece in enumerate(split3(dense)):
        for k in range(dense.shape[0]):
            lanes = slice(first + k * LANES, first + (k + 1) * LANES)
            wide_ref[at + p : at + p + 1, lanes] = piece[k : k + 1, :]
    turn(wide_ref, rows_ref, first, first + cells)


def halves_of(cells):
    parts = math.gcd(2, max(cells // (8 * LANES), 1))
    return [(p * (cells // parts), (p + 1) * (cells // parts)) for p in range(parts)]


def join(peak, total, block):
    t = block.reshape(-1, 8, LANES)
    newpeak = jnp.maximum(peak, jnp.max(t, axis=0))
    total = total * jnp.exp2(peak - newpeak) + jnp.sum(jnp.exp2(t - newpeak[None]), axis=0)
    return newpeak, total


def closed(peak, total):
    top = jnp.max(peak, axis=0, keepdims=True)
    return top, jnp.sum(total * jnp.exp2(peak - top), axis=0, keepdims=True)


def lse_pass(rows_ref, columns_ref, stats_ref, lse_ref, row_span, lane_span, fresh):
    (low, high), (begin, end) = row_span, lane_span
    width = math.gcd(end - begin, WIDTH)
    step = math.gcd(high - low, STEP)
    sub = math.gcd(step, SUB)
    halves = width // LANES

    def over_columns(c, unused):
        right = columns_ref[:, pl.ds(pl.multiple_of(begin + c * width, width), width)]
        tiles = [begin // LANES + c * halves + h for h in range(halves)]
        if fresh:
            empty = (jnp.full((8, LANES), -jnp.inf, jnp.float32), jnp.zeros((8, LANES), jnp.float32))
            stats = [empty] * halves
        else:
            stats = [(stats_ref[0, tile], stats_ref[1, tile]) for tile in tiles]
        for r in range((high - low) // step):
            block = jnp.dot(
                rows_ref[low + r * step : low + (r + 1) * step, :], right,
                preferred_element_type=jnp.float32,
            )
            for q in range(step // sub):
                for h in range(halves):
                    cut = block[q * sub : (q + 1) * sub, h * LANES : (h + 1) * LANES]
                    stats[h] = join(*stats[h], cut)
        for tile, (peak, total) in zip(tiles, stats):
            if lse_ref is None:
                stats_ref[0, tile] = peak
                stats_ref[1, tile] = total
            else:
                top, total = closed(peak, total)
                lse_ref[pl.ds(tile, 1), :] = top + jnp.log2(total)
        return unused

    lax.fori_loop(0, (end - begin) // width, over_columns, 0, unroll=True)


def fill_tile(rows_ref, right, tile_ref, row_span, peak):
    low, high = row_span
    width = tile_ref.shape[1]
    step = math.gcd(high - low, STEP)
    for r in range((high - low) // step):
        at = slice(low + r * step, low + (r + 1) * step)
        block = jnp.dot(rows_ref[at, :], right, preferred_element_type=jnp.float32)
        tile_ref[at, :] = block
        peak = jnp.maximum(peak, jnp.max(block.reshape(-1, 8, width), axis=0))
    return peak


def carry_tile(tile_ref, peak, scores_ref, weights):
    rows = tile_ref.shape[0]
    step = math.gcd(rows, STEP)
    for r in range(rows // step):
        at = slice(r * step, (r + 1) * step)
        weights[at, :] = jnp.exp2(tile_ref[at, :] - peak).astype(jnp.bfloat16)
    return jnp.dot(scores_ref[...], weights[...], preferred_element_type=jnp.float32)


def kernel(
    n_src, n_tgt, xs_ref, yt_ref, growth_ref, scores_ref, f_ref, g_ref, out_ref,
    tile, x_wide, y_wide, x_rows, x_cols, y_rows, y_cols, scores_t, weights, running, sums, peaks, pay,
    row_buf, col_buf, f_all, g_all, row_send, row_recv, col_send, col_recv,
    bulk_send, bulk_recv, pass_send, pass_recv, f_send, f_recv, out_send, out_recv,
):
    src, tgt = lax.axis_index("src"), lax.axis_index("tgt")
    barrier = pltpu.get_barrier_semaphore()
    for k in range(1, n_src):
        pl.semaphore_signal(
            barrier, inc=1, device_id={"src": lax.rem(src + k, n_src)}, device_id_type=MESH
        )
    for k in range(1, n_tgt):
        pl.semaphore_signal(
            barrier, inc=1, device_id={"tgt": lax.rem(tgt + k, n_tgt)}, device_id_type=MESH
        )

    pcs, rows = xs_ref.shape
    columns = yt_ref.shape[1]
    programs = scores_ref.shape[1]
    scale = 2.0 * LOG2E / (pcs * EPSILON)
    bias_at = 3 * depth_of(pcs)[0] + 8
    augment(yt_ref[...], y_wide, scale, False)
    y_cols[...] = y_wide[...].astype(jnp.bfloat16)
    turn(y_wide, y_rows, 0, columns)
    augment(xs_ref[...], x_wide.at[0], scale, True)
    x_cols[...] = x_wide[0].astype(jnp.bfloat16)

    pay[0, programs:, :] = jnp.zeros((pay.shape[1] - programs, rows), jnp.float32)
    pay[0, programs : programs + pcs, :] = xs_ref[...].astype(jnp.float32)
    for k in range(rows // LANES):
        cut = slice(k * LANES, (k + 1) * LANES)
        pay[0, 0:programs, cut] = scores_ref[cut, :].astype(jnp.float32).T
    scores_t[0, 0:programs, :] = pay[0, 0:programs, :].astype(jnp.bfloat16)
    for p in range(scores_t.shape[0]):
        scores_t[p, programs:, :] = jnp.ones((16, rows), jnp.bfloat16)

    bits = [1 << b for b in range(n_src.bit_length() - 1)]
    core, share = lax.rem(tgt, 2), pay.shape[1] // 4

    def relative(mask):
        there = src
        for bit in bits:
            if mask & bit:
                there = there + bit - 2 * bit * lax.rem(lax.div(src, bit), 2)
        return there

    early = share // 3 // 8 * 8
    spans_of_share = [(0, early), (early, share)] if early else [(0, share)]
    parts = range(len(spans_of_share))

    def lines_at(order, part):
        low, high = spans_of_share[part]
        return pl.ds(pl.multiple_of((2 * core + order) * share + low, 8), high - low)

    bulk, passed = {}, {}

    def ship(order, bit, mask, part):
        lines, there = lines_at(order, part), mask ^ bit
        copy = pltpu.make_async_remote_copy(
            src_ref=pay.at[mask, lines], dst_ref=pay.at[there, lines],
            send_sem=bulk_send.at[order, there, part], recv_sem=bulk_recv.at[order, there, part],
            device_id={"src": relative(bit)}, device_id_type=MESH,
        )
        copy.start()
        bulk[order, there, part] = copy

    def hand_over(mask, chosen=(0, 1)):
        for part in parts:
            for order in chosen:
                if (order, mask, part) in passed:
                    continue
                bulk[order, mask, part].wait_recv()
                lines = lines_at(order, part)
                copy = pltpu.make_async_remote_copy(
                    src_ref=pay.at[mask, lines], dst_ref=pay.at[mask, lines],
                    send_sem=pass_send.at[order, mask, part],
                    recv_sem=pass_recv.at[order, mask, part],
                    device_id={"tgt": tgt + 1 - 2 * core}, device_id_type=MESH,
                )
                copy.start()
                passed[order, mask, part] = copy

    orders = [bits, bits[::-1]]

    def ship_own(stages, chosen):
        for t in stages:
            for part in chosen:
                for order, bit in enumerate(orders):
                    ship(order, bit[t], 0, part)

    def ship_rest():
        for order, bit in enumerate(orders):
            hand_over(bit[0], (order,))
        for t in range(1, len(bits)):
            for order, bit in enumerate(orders):
                held = [0]
                for b in bit[:t]:
                    held += [m ^ b for m in held]
                for mask in held[1:]:
                    hand_over(mask, (order,))
                    for part in parts:
                        ship(order, bit[t], mask, part)

    def exchange(buf, axis, me, n, send, recv, lines):
        copies = [
            pltpu.make_async_remote_copy(
                src_ref=buf.at[me, lines], dst_ref=buf.at[me, lines],
                send_sem=send.at[k], recv_sem=recv.at[k],
                device_id={axis: lax.rem(me + k, n)}, device_id_type=MESH,
            )
            for k in range(1, n)
        ]
        for copy in copies:
            copy.start()
        return copies

    def joined(buf, n, lines):
        parts = [buf[d, lines] for d in range(n)]
        top = functools.reduce(jnp.maximum, parts)
        return top + jnp.log2(sum(jnp.exp2(part - top) for part in parts))

    log_a = jnp.log2(growth_ref[...]) - math.log2(rows * n_src)
    log_b = -math.log2(columns * n_tgt)
    quarters = n_src == 4
    source_halves, target_halves = halves_of(rows), halves_of(columns)

    def lines_of(span):
        return slice(span[0] // LANES, span[1] // LANES)

    def finish(rows_ref, columns_ref, row_span, spans, fresh, buf, axis, me, n, send, recv):
        sent = []
        for h, span in enumerate(spans):
            lse_pass(rows_ref, columns_ref, running, buf.at[me], row_span, span, fresh)
            sent.append(exchange(buf, axis, me, n, send.at[h], recv.at[h], lines_of(span)))
        return sent

    def settle(copies):
        for copy in copies:
            copy.wait()

    for step in range(ITERS):
        over_tgt = (row_buf.at[step], "tgt", tgt, n_tgt, row_send.at[step], row_recv.at[step])
        over_src = (col_buf.at[step], "src", src, n_src, col_send.at[step], col_recv.at[step])
        if step == 0:
            pl.semaphore_wait(barrier, n_src + n_tgt - 2)
            ship_own(range(1), parts)
            ship_own(range(1, len(bits)), parts[:1])
            sent = finish(y_rows, x_cols, (0, columns), source_halves, True, *over_tgt)
        else:
            for h, span in enumerate(target_halves):
                settle(sent[h])
                lines = lines_of(span)
                g = FACTOR * (log_b - joined(col_buf.at[step - 1], n_src, lines))
                set_bias(g, y_wide, y_rows, bias_at + 3, span[0])
                if h < len(target_halves) - 1:
                    lse_pass(y_rows, x_cols, running, None, span, (0, rows), h == 0)
            sent = finish(y_rows, x_cols, span, source_halves, h == 0, *over_tgt)
        if step == ITERS - 1:
            break
        for h, span in enumerate(source_halves):
            settle(sent[h])
            lines = lines_of(span)
            f = FACTOR * (log_a[lines] - joined(row_buf.at[step], n_tgt, lines))
            set_bias(f, x_wide.at[0], x_rows.at[0], bias_at, span[0])
            if h < len(source_halves) - 1:
                lse_pass(x_rows.at[0], y_cols, running, None, span, (0, columns), h == 0)
        sent = finish(x_rows.at[0], y_cols, span, target_halves, h == 0, *over_src)
        if step == 0:
            ship_own(range(1, len(bits)), parts[1:])
            if quarters:
                ship_rest()

    width, slots = tile.shape[2], x_rows.shape[0]
    groups, halves = columns // width, width // LANES
    piece = columns // n_src
    empty = jnp.full((8, width), -jnp.inf, jnp.float32)

    def fill(block, start, slot, span, peak):
        right = y_cols[:, pl.ds(pl.multiple_of(start, width), width)]
        return fill_tile(x_rows.at[block % slots], right, tile.at[slot], span, peak)

    def unpack(block):
        hand_over(block)
        for order in range(2):
            for part in parts:
                passed[order, block, part].wait_recv()
        augment(pay[block, programs : programs + pcs, :], x_wide.at[block % slots], scale, True)
        scores_t[block % slots, 0:programs, :] = pay[block, 0:programs, :].astype(jnp.bfloat16)

    def admit(block):
        shared[block].wait_recv()
        slot = block % slots
        set_bias(f_all[block], x_wide.at[slot], x_rows.at[slot], bias_at, 0)

    def carry(block, start, place, slot, ready):
        peak = jnp.max(ready, axis=0, keepdims=True)
        if block > 0:
            before = peaks[place, 0:1, :]
            peak = jnp.maximum(peak, before)
        carried = carry_tile(tile.at[slot], peak, scores_t.at[block % slots], weights.at[slot])
        if block > 0:
            carried = carried + sums[place] * jnp.exp2(before - peak)
        if block < n_src - 1:
            sums[place] = carried
            peaks[place, 0:1, :] = peak
            return
        mass = carried[programs : programs + 1, :]
        g = UNIT * FACTOR * (log_b - (peak + jnp.log2(mass)))
        carried = carried[0:programs, :] / mass
        for h in range(halves):
            cut = slice(h * LANES, (h + 1) * LANES)
            at = start + h * LANES
            owner = lax.div(at, piece)
            g_all[owner, pl.ds(lax.div(at - owner * piece, LANES), 1), :] = g[:, cut]
            out_ref[pl.ds(pl.multiple_of(at, LANES), LANES), :] = carried[:, cut].T

    if quarters:
        for block in range(1, n_src - 1):
            hand_over(block)
        for block in range(1, n_src - 1):
            unpack(block)
    ready, shared = empty, {}
    for h, span in enumerate(source_halves):
        settle(sent[h])
        lines = lines_of(span)
        f = FACTOR * (log_a[lines] - joined(row_buf.at[ITERS - 1], n_tgt, lines))
        f_ref[lines, :] = UNIT * f
        f_all[0, lines, :] = f
        if h == len(source_halves) - 1:
            for mask in range(1, n_src):
                shared[mask] = pltpu.make_async_remote_copy(
                    src_ref=f_all.at[0], dst_ref=f_all.at[mask],
                    send_sem=f_send.at[mask], recv_sem=f_recv.at[mask],
                    device_id={"src": relative(mask)}, device_id_type=MESH,
                )
                shared[mask].start()
            if not quarters:
                ship_rest()
        set_bias(f, x_wide.at[0], x_rows.at[0], bias_at, span[0])
        if quarters:
            ready = fill(0, src * piece, 0, span, ready)

    gathered = []
    if quarters:
        wide = piece // width
        mine = [(src * piece + c * width, c) for c in range(wide)]
        spare = [((3 - src) * piece + c * width, wide + c) for c in range(wide)]
        order = [(0, spot) for spot in mine + spare]
        order += [(block, spot) for block in range(1, n_src) for spot in mine]
        order += [(block, spot) for block in range(1, n_src) for spot in spare]
        for u, (block, spot) in enumerate(order):
            now, after = ready, order[u + 1] if u + 1 < len(order) else None
            fresh = after and after[0] > block and u < 2 * wide + (n_src - 1) * wide - 1
            if fresh and after[0] == 1:
                carry(block, *spot, u % 2, now)
                now = None
                hand_over(n_src - 1)
            if fresh:
                if after[0] == n_src - 1:
                    unpack(after[0])
                admit(after[0])
            if after:
                ready = fill(after[0], after[1][0], (u + 1) % 2, (0, rows), empty)
            if now is not None:
                carry(block, *spot, u % 2, now)
            if u == 2 * wide + (n_src - 1) * wide - 1:
                at = pl.ds(pl.multiple_of(src * piece, piece), piece)
                for k, bit in enumerate(bits):
                    for slot, ref in enumerate((out_ref.at[at, :], g_all.at[src])):
                        copy = pltpu.make_async_remote_copy(
                            src_ref=ref, dst_ref=ref,
                            send_sem=out_send.at[slot, k], recv_sem=out_recv.at[slot, k],
                            device_id={"src": relative(bit)}, device_id_type=MESH,
                        )
                        copy.start()
                        gathered.append(copy)
    else:
        for block in range(n_src):
            if block > 0:
                unpack(block)
                admit(block)

            def over_groups(c, unused, block=block):
                start = c * width
                carry(block, start, c, 0, fill(block, start, 0, (0, rows), empty))
                return unused

            lax.fori_loop(0, groups, over_groups, 0)
    for copy in gathered:
        copy.wait()
    for k in range(n_src):
        g_ref[k * (piece // LANES) : (k + 1) * (piece // LANES), :] = g_all[k, 0 : piece // LANES, :]
    for copy in [*bulk.values(), *passed.values(), *shared.values()]:
        copy.wait_send()


def deliver(f_ref, g_ref, out_ref, f_end, g_end, out_end, sems):
    refs = ((f_ref, f_end), (g_ref, g_end), (out_ref, out_end))
    copies = [pltpu.make_async_copy(a, b, sems.at[k]) for k, (a, b) in enumerate(refs)]
    for copy in copies:
        copy.start()
    for copy in copies:
        copy.wait()


def solution(mesh):
    n_src, n_tgt = mesh.shape["src"], mesh.shape["tgt"]

    def shards(pcs_source, pcs_target, growth, scores):
        rows, columns = pcs_source.shape[1], pcs_target.shape[1]
        programs = scores.shape[1]
        width, slots = math.gcd(columns, WIDTH), 2
        if n_src == 4:
            width, slots = math.gcd(columns // n_src, WIDTH), n_src
        pcs = pcs_source.shape[0]
        depth = depth_of(pcs)[1]
        f32, bf16 = jnp.float32, jnp.bfloat16
        sem = pltpu.SemaphoreType.DMA
        whole = pl.BlockSpec(memory_space=pltpu.VMEM)
        dense_r, dense_c = (rows // LANES, LANES), (columns // LANES, LANES)
        shapes = (
            pltpu.VMEM(dense_r, f32), pltpu.VMEM(dense_c, f32), pltpu.VMEM((columns, programs), f32)
        )
        results = pl.pallas_call(
            functools.partial(kernel, n_src, n_tgt),
            out_shape=shapes,
            in_specs=[whole] * 4,
            out_specs=(whole,) * 3,
            scratch_shapes=[
                pltpu.VMEM((2, rows, width), f32),
                pltpu.VMEM((slots, depth, rows), f32),
                pltpu.VMEM((depth, columns), f32),
                pltpu.VMEM((slots, rows, depth), bf16),
                pltpu.VMEM((depth, rows), bf16),
                pltpu.VMEM((columns, depth), bf16),
                pltpu.VMEM((depth, columns), bf16),
                pltpu.VMEM((slots, programs + 16, rows), bf16),
                pltpu.VMEM((2, rows, width), bf16),
                pltpu.VMEM((2, max(rows, columns) // LANES, 8, LANES), f32),
                pltpu.VMEM((columns // width, programs + 16, width), f32),
                pltpu.VMEM((columns // width, 8, width), f32),
                pltpu.VMEM((n_src, -(-(programs + pcs) // 32) * 32, rows), f32),
                pltpu.VMEM((ITERS, n_tgt) + dense_r, f32),
                pltpu.VMEM((ITERS, n_src) + dense_c, f32),
                pltpu.VMEM((n_src,) + dense_r, f32),
                pltpu.VMEM((n_src, -(-columns // n_src // (8 * LANES)) * 8, LANES), f32),
                sem((ITERS, 2, n_tgt)),
                sem((ITERS, 2, n_tgt)),
                sem((ITERS, 2, n_src)),
                sem((ITERS, 2, n_src)),
                sem((2, n_src, 2)),
                sem((2, n_src, 2)),
                sem((2, n_src, 2)),
                sem((2, n_src, 2)),
                sem((n_src,)),
                sem((n_src,)),
                sem((2, 2)),
                sem((2, 2)),
            ],
            compiler_params=pltpu.CompilerParams(
                collective_id=0, has_side_effects=True, vmem_limit_bytes=60 * 2**20
            ),
            name="coupling",
        )(pcs_source, pcs_target, growth.reshape(dense_r), scores)
        f, g, out = pl.pallas_call(
            deliver,
            out_shape=tuple(jax.ShapeDtypeStruct(shape.shape, f32) for shape in shapes),
            in_specs=[whole] * 3,
            out_specs=(pl.BlockSpec(memory_space=pl.ANY),) * 3,
            scratch_shapes=[sem((3,))],
            name="deliver",
        )(*[pltpu.with_memory_space_constraint(result, pltpu.VMEM) for result in results])
        return f.reshape(-1), g.reshape(-1), out

    in_specs = (P(None, "src"), P(None, "tgt"), P("src"), P("src", None))
    out_specs = (P("src"), P("tgt"), P("tgt", None))
    return jax.shard_map(shards, mesh=mesh, in_specs=in_specs, out_specs=out_specs, check_vma=False)
```

```python
import functools
import math

import jax
import jax.numpy as jnp
from jax import lax
from jax.experimental import pallas as pl
from jax.experimental.pallas import tpu as pltpu
from jax.sharding import PartitionSpec as P

ITERS = 2
EPSILON = 0.05
MARGIN = 1.0
FACTOR = MARGIN / (MARGIN + EPSILON)
LANES = 128
LOG2E = math.log2(math.e)
UNIT = EPSILON / LOG2E
MESH = pl.DeviceIdType.MESH
WIDTH, STEP, SUB = 512, 256, 64


def split3(value):
    high = value.astype(jnp.bfloat16).astype(jnp.float32)
    mid = (value - high).astype(jnp.bfloat16).astype(jnp.float32)
    return high, mid, value - high - mid


def depth_of(pcs):
    base = -(-pcs // 8) * 8
    return base, -(-(3 * base + 16) // LANES) * LANES


def augment(coords, wide_ref, scale, source):
    pcs, cells = coords.shape
    base, depth = depth_of(pcs)
    wide = coords.astype(jnp.float32)
    norm = -0.5 * scale * jnp.sum(wide * wide, axis=0, keepdims=True)
    at = lax.broadcasted_iota(jnp.int32, (16, cells), 0) - (0 if source else 3)
    high, mid, low = split3(norm)
    extra = jnp.where(at == 0, high, jnp.where(at == 1, mid, jnp.where(at == 2, low, 0.0)))
    at = lax.broadcasted_iota(jnp.int32, (16, cells), 0)
    ones = ((at >= 3) & (at < 6)) | ((at >= 11) & (at < 14)) if source else (at < 3) | ((at >= 8) & (at < 11))
    wide_ref[...] = jnp.zeros(wide_ref.shape, jnp.float32)
    for k, piece in enumerate(split3(scale * wide) if source else (wide,) * 3):
        wide_ref[k * base : k * base + pcs, :] = piece
    wide_ref[3 * base : 3 * base + 16, :] = jnp.where(ones, 1.0, extra)


def turn(wide_ref, rows_ref, first, last):
    depth = wide_ref.shape[0]
    for k in range(first // LANES, last // LANES):
        cut = slice(k * LANES, (k + 1) * LANES)
        for d in range(depth // LANES):
            deep = slice(d * LANES, (d + 1) * LANES)
            rows_ref[cut, deep] = wide_ref[deep, cut].T.astype(jnp.bfloat16)


def set_bias(dense, wide_ref, rows_ref, at, first):
    cells = dense.shape[0] * LANES
    for p, piece in enumerate(split3(dense)):
        for k in range(dense.shape[0]):
            lanes = slice(first + k * LANES, first + (k + 1) * LANES)
            wide_ref[at + p : at + p + 1, lanes] = piece[k : k + 1, :]
    turn(wide_ref, rows_ref, first, first + cells)


def halves_of(cells):
    parts = math.gcd(2, max(cells // (8 * LANES), 1))
    return [(p * (cells // parts), (p + 1) * (cells // parts)) for p in range(parts)]


def join(peak, total, block):
    t = block.reshape(-1, 8, LANES)
    newpeak = jnp.maximum(peak, jnp.max(t, axis=0))
    total = total * jnp.exp2(peak - newpeak) + jnp.sum(jnp.exp2(t - newpeak[None]), axis=0)
    return newpeak, total


def closed(peak, total):
    top = jnp.max(peak, axis=0, keepdims=True)
    return top, jnp.sum(total * jnp.exp2(peak - top), axis=0, keepdims=True)


def lse_pass(rows_ref, columns_ref, stats_ref, lse_ref, row_span, lane_span, fresh):
    (low, high), (begin, end) = row_span, lane_span
    width = math.gcd(end - begin, WIDTH)
    step = math.gcd(high - low, STEP)
    sub = math.gcd(step, SUB)
    halves = width // LANES

    def over_columns(c, unused):
        right = columns_ref[:, pl.ds(pl.multiple_of(begin + c * width, width), width)]
        tiles = [begin // LANES + c * halves + h for h in range(halves)]
        if fresh:
            empty = (jnp.full((8, LANES), -jnp.inf, jnp.float32), jnp.zeros((8, LANES), jnp.float32))
            stats = [empty] * halves
        else:
            stats = [(stats_ref[0, tile], stats_ref[1, tile]) for tile in tiles]
        for r in range((high - low) // step):
            block = jnp.dot(
                rows_ref[low + r * step : low + (r + 1) * step, :], right,
                preferred_element_type=jnp.float32,
            )
            for q in range(step // sub):
                for h in range(halves):
                    cut = block[q * sub : (q + 1) * sub, h * LANES : (h + 1) * LANES]
                    stats[h] = join(*stats[h], cut)
        for tile, (peak, total) in zip(tiles, stats):
            if lse_ref is None:
                stats_ref[0, tile] = peak
                stats_ref[1, tile] = total
            else:
                top, total = closed(peak, total)
                lse_ref[pl.ds(tile, 1), :] = top + jnp.log2(total)
        return unused

    lax.fori_loop(0, (end - begin) // width, over_columns, 0, unroll=True)


def fill_tile(rows_ref, right, tile_ref, row_span, peak):
    low, high = row_span
    width = tile_ref.shape[1]
    step = math.gcd(high - low, STEP)
    for r in range((high - low) // step):
        at = slice(low + r * step, low + (r + 1) * step)
        block = jnp.dot(rows_ref[at, :], right, preferred_element_type=jnp.float32)
        tile_ref[at, :] = block
        peak = jnp.maximum(peak, jnp.max(block.reshape(-1, 8, width), axis=0))
    return peak


def carry_tile(tile_ref, peak, scores_ref, weights):
    rows = tile_ref.shape[0]
    step = math.gcd(rows, STEP)
    for r in range(rows // step):
        at = slice(r * step, (r + 1) * step)
        weights[at, :] = jnp.exp2(tile_ref[at, :] - peak).astype(jnp.bfloat16)
    return jnp.dot(scores_ref[...], weights[...], preferred_element_type=jnp.float32)


def kernel(
    n_src, n_tgt, xs_ref, yt_ref, growth_ref, scores_ref, f_ref, g_ref, out_ref,
    tile, x_wide, y_wide, x_rows, x_cols, y_rows, y_cols, scores_t, weights, running, sums, peaks, pay,
    row_buf, col_buf, f_all, g_all, row_send, row_recv, col_send, col_recv,
    bulk_send, bulk_recv, pass_send, pass_recv, f_send, f_recv, out_send, out_recv,
):
    src, tgt = lax.axis_index("src"), lax.axis_index("tgt")
    barrier = pltpu.get_barrier_semaphore()
    for k in range(1, n_src):
        pl.semaphore_signal(
            barrier, inc=1, device_id={"src": lax.rem(src + k, n_src)}, device_id_type=MESH
        )
    for k in range(1, n_tgt):
        pl.semaphore_signal(
            barrier, inc=1, device_id={"tgt": lax.rem(tgt + k, n_tgt)}, device_id_type=MESH
        )

    pcs, rows = xs_ref.shape
    columns = yt_ref.shape[1]
    programs = scores_ref.shape[1]
    scale = 2.0 * LOG2E / (pcs * EPSILON)
    bias_at = 3 * depth_of(pcs)[0] + 8
    augment(yt_ref[...], y_wide, scale, False)
    y_cols[...] = y_wide[...].astype(jnp.bfloat16)
    turn(y_wide, y_rows, 0, columns)
    augment(xs_ref[...], x_wide.at[0], scale, True)
    x_cols[...] = x_wide[0].astype(jnp.bfloat16)

    pay[0, programs:, :] = jnp.zeros((pay.shape[1] - programs, rows), jnp.float32)
    pay[0, programs : programs + pcs, :] = xs_ref[...].astype(jnp.float32)
    for k in range(rows // LANES):
        cut = slice(k * LANES, (k + 1) * LANES)
        pay[0, 0:programs, cut] = scores_ref[cut, :].astype(jnp.float32).T
    scores_t[0, 0:programs, :] = pay[0, 0:programs, :].astype(jnp.bfloat16)
    for p in range(scores_t.shape[0]):
        scores_t[p, programs:, :] = jnp.ones((16, rows), jnp.bfloat16)

    bits = [1 << b for b in range(n_src.bit_length() - 1)]
    core, share = lax.rem(tgt, 2), pay.shape[1] // 4

    def relative(mask):
        there = src
        for bit in bits:
            if mask & bit:
                there = there + bit - 2 * bit * lax.rem(lax.div(src, bit), 2)
        return there

    early = max(share // 5 // 8 * 8, 8)
    marks = [0, early, max(share - early, early), share]
    spans_of_share = list(zip(marks, marks[1:]))
    parts = range(len(spans_of_share))

    def lines_at(order, part):
        low, high = spans_of_share[part]
        return pl.ds(pl.multiple_of((2 * core + order) * share + low, 8), high - low)

    bulk, passed = {}, {}

    def ship(order, bit, mask, part):
        lines, there = lines_at(order, part), mask ^ bit
        copy = pltpu.make_async_remote_copy(
            src_ref=pay.at[mask, lines], dst_ref=pay.at[there, lines],
            send_sem=bulk_send.at[order, there, part], recv_sem=bulk_recv.at[order, there, part],
            device_id={"src": relative(bit)}, device_id_type=MESH,
        )
        copy.start()
        bulk[order, there, part] = copy

    def hand_over(mask, chosen=(0, 1), pieces=parts):
        for part in pieces:
            for order in chosen:
                if (order, mask, part) in passed:
                    continue
                bulk[order, mask, part].wait_recv()
                lines = lines_at(order, part)
                copy = pltpu.make_async_remote_copy(
                    src_ref=pay.at[mask, lines], dst_ref=pay.at[mask, lines],
                    send_sem=pass_send.at[order, mask, part],
                    recv_sem=pass_recv.at[order, mask, part],
                    device_id={"tgt": tgt + 1 - 2 * core}, device_id_type=MESH,
                )
                copy.start()
                passed[order, mask, part] = copy

    orders = [bits, bits[::-1]]

    def ship_own(stages, chosen):
        for t in stages:
            for part in chosen:
                for order, bit in enumerate(orders):
                    ship(order, bit[t], 0, part)

    def ship_rest(chosen):
        for order, bit in enumerate(orders):
            hand_over(bit[0], (order,))
        for t in range(1, len(bits)):
            for order, bit in enumerate(orders):
                held = [0]
                for b in bit[:t]:
                    held += [m ^ b for m in held]
                for mask in held[1:]:
                    hand_over(mask, (order,))
                    for part in chosen:
                        ship(order, bit[t], mask, part)

    def exchange(buf, axis, me, n, send, recv, lines):
        copies = [
            pltpu.make_async_remote_copy(
                src_ref=buf.at[me, lines], dst_ref=buf.at[me, lines],
                send_sem=send.at[k], recv_sem=recv.at[k],
                device_id={axis: lax.rem(me + k, n)}, device_id_type=MESH,
            )
            for k in range(1, n)
        ]
        for copy in copies:
            copy.start()
        return copies

    def joined(buf, n, lines):
        parts = [buf[d, lines] for d in range(n)]
        top = functools.reduce(jnp.maximum, parts)
        return top + jnp.log2(sum(jnp.exp2(part - top) for part in parts))

    log_a = jnp.log2(growth_ref[...]) - math.log2(rows * n_src)
    log_b = -math.log2(columns * n_tgt)
    quarters = n_src == 4
    source_halves, target_halves = halves_of(rows), halves_of(columns)

    def lines_of(span):
        return slice(span[0] // LANES, span[1] // LANES)

    def finish(rows_ref, columns_ref, row_span, spans, fresh, buf, axis, me, n, send, recv):
        sent = []
        for h, span in enumerate(spans):
            lse_pass(rows_ref, columns_ref, running, buf.at[me], row_span, span, fresh)
            sent.append(exchange(buf, axis, me, n, send.at[h], recv.at[h], lines_of(span)))
        return sent

    def settle(copies):
        for copy in copies:
            copy.wait()

    for step in range(ITERS):
        over_tgt = (row_buf.at[step], "tgt", tgt, n_tgt, row_send.at[step], row_recv.at[step])
        over_src = (col_buf.at[step], "src", src, n_src, col_send.at[step], col_recv.at[step])
        if step == 0:
            pl.semaphore_wait(barrier, n_src + n_tgt - 2)
            ship_own(range(1), parts)
            ship_own(range(1, len(bits)), parts[:1])
            sent = finish(y_rows, x_cols, (0, columns), source_halves, True, *over_tgt)
        else:
            for h, span in enumerate(target_halves):
                settle(sent[h])
                lines = lines_of(span)
                g = FACTOR * (log_b - joined(col_buf.at[step - 1], n_src, lines))
                set_bias(g, y_wide, y_rows, bias_at + 3, span[0])
                if h < len(target_halves) - 1:
                    lse_pass(y_rows, x_cols, running, None, span, (0, rows), h == 0)
            sent = finish(y_rows, x_cols, span, source_halves, h == 0, *over_tgt)
        if step == ITERS - 1:
            break
        for h, span in enumerate(source_halves):
            settle(sent[h])
            lines = lines_of(span)
            f = FACTOR * (log_a[lines] - joined(row_buf.at[step], n_tgt, lines))
            set_bias(f, x_wide.at[0], x_rows.at[0], bias_at, span[0])
            if h < len(source_halves) - 1:
                lse_pass(x_rows.at[0], y_cols, running, None, span, (0, columns), h == 0)
        sent = finish(x_rows.at[0], y_cols, span, target_halves, h == 0, *over_src)
        if step == 0:
            ship_own(range(1, len(bits)), parts[1:])
            if quarters:
                ship_rest(parts[:-1])

    width, slots = tile.shape[2], x_rows.shape[0]
    groups, halves = columns // width, width // LANES
    piece = columns // n_src
    empty = jnp.full((8, width), -jnp.inf, jnp.float32)

    def fill(block, start, slot, span, peak):
        right = y_cols[:, pl.ds(pl.multiple_of(start, width), width)]
        return fill_tile(x_rows.at[block % slots], right, tile.at[slot], span, peak)

    def unpack(block):
        hand_over(block)
        for order in range(2):
            for part in parts:
                passed[order, block, part].wait_recv()
        augment(pay[block, programs : programs + pcs, :], x_wide.at[block % slots], scale, True)
        scores_t[block % slots, 0:programs, :] = pay[block, 0:programs, :].astype(jnp.bfloat16)

    def admit(block):
        shared[block].wait_recv()
        slot = block % slots
        set_bias(f_all[block], x_wide.at[slot], x_rows.at[slot], bias_at, 0)

    def carry(block, start, place, slot, ready):
        peak = jnp.max(ready, axis=0, keepdims=True)
        if block > 0:
            before = peaks[place, 0:1, :]
            peak = jnp.maximum(peak, before)
        carried = carry_tile(tile.at[slot], peak, scores_t.at[block % slots], weights.at[slot])
        if block > 0:
            carried = carried + sums[place] * jnp.exp2(before - peak)
        if block < n_src - 1:
            sums[place] = carried
            peaks[place, 0:1, :] = peak
            return
        mass = carried[programs : programs + 1, :]
        g = UNIT * FACTOR * (log_b - (peak + jnp.log2(mass)))
        carried = carried[0:programs, :] / mass
        for h in range(halves):
            cut = slice(h * LANES, (h + 1) * LANES)
            at = start + h * LANES
            owner = lax.div(at, piece)
            g_all[owner, pl.ds(lax.div(at - owner * piece, LANES), 1), :] = g[:, cut]
            out_ref[pl.ds(pl.multiple_of(at, LANES), LANES), :] = carried[:, cut].T

    if quarters:
        for block in range(1, n_src - 1):
            hand_over(block)
        for block in range(1, n_src - 1):
            unpack(block)
    ready, shared = empty, {}
    for h, span in enumerate(source_halves):
        settle(sent[h])
        lines = lines_of(span)
        f = FACTOR * (log_a[lines] - joined(row_buf.at[ITERS - 1], n_tgt, lines))
        f_ref[lines, :] = UNIT * f
        f_all[0, lines, :] = f
        if h == len(source_halves) - 1:
            for mask in range(1, n_src):
                shared[mask] = pltpu.make_async_remote_copy(
                    src_ref=f_all.at[0], dst_ref=f_all.at[mask],
                    send_sem=f_send.at[mask], recv_sem=f_recv.at[mask],
                    device_id={"src": relative(mask)}, device_id_type=MESH,
                )
                shared[mask].start()
            ship_rest(parts[-1:] if quarters else parts)
        set_bias(f, x_wide.at[0], x_rows.at[0], bias_at, span[0])
        if quarters:
            ready = fill(0, src * piece, 0, span, ready)

    gathered = []
    if quarters:
        wide = piece // width
        mine = [(src * piece + c * width, c) for c in range(wide)]
        spare = [((3 - src) * piece + c * width, wide + c) for c in range(wide)]
        order = [(0, spot) for spot in mine + spare]
        order += [(block, spot) for spot in mine + spare for block in range(1, n_src)]
        for u, (block, spot) in enumerate(order):
            now, after = ready, order[u + 1] if u + 1 < len(order) else None
            fresh = after and after[0] > block and after[1][1] == 0
            if fresh and after[0] == 1:
                carry(block, *spot, u % 2, now)
                now = None
                hand_over(n_src - 1, pieces=parts[:-1])
            if fresh:
                if after[0] == n_src - 2:
                    hand_over(n_src - 1)
                if after[0] == n_src - 1:
                    unpack(after[0])
                admit(after[0])
            if after:
                ready = fill(after[0], after[1][0], (u + 1) % 2, (0, rows), empty)
            if now is not None:
                carry(block, *spot, u % 2, now)
            if block == n_src - 1 and spot[1] < wide:
                at = pl.ds(pl.multiple_of(spot[0], width), width)
                refs = [out_ref.at[at, :]] + [g_all.at[src]] * (spot[1] == wide - 1)
                for k, bit in enumerate(bits):
                    for slot, ref in enumerate(refs):
                        where = spot[1] if slot == 0 else wide
                        copy = pltpu.make_async_remote_copy(
                            src_ref=ref, dst_ref=ref,
                            send_sem=out_send.at[where, k], recv_sem=out_recv.at[where, k],
                            device_id={"src": relative(bit)}, device_id_type=MESH,
                        )
                        copy.start()
                        gathered.append(copy)
    else:
        for block in range(n_src):
            if block > 0:
                unpack(block)
                admit(block)

            def over_groups(c, unused, block=block):
                start = c * width
                carry(block, start, c, 0, fill(block, start, 0, (0, rows), empty))
                return unused

            lax.fori_loop(0, groups, over_groups, 0)
    for copy in gathered:
        copy.wait()
    for k in range(n_src):
        g_ref[k * (piece // LANES) : (k + 1) * (piece // LANES), :] = g_all[k, 0 : piece // LANES, :]
    for copy in [*bulk.values(), *passed.values(), *shared.values()]:
        copy.wait_send()


def deliver(f_ref, g_ref, out_ref, f_end, g_end, out_end, sems):
    refs = ((f_ref, f_end), (g_ref, g_end), (out_ref, out_end))
    copies = [pltpu.make_async_copy(a, b, sems.at[k]) for k, (a, b) in enumerate(refs)]
    for copy in copies:
        copy.start()
    for copy in copies:
        copy.wait()


def solution(mesh):
    n_src, n_tgt = mesh.shape["src"], mesh.shape["tgt"]

    def shards(pcs_source, pcs_target, growth, scores):
        rows, columns = pcs_source.shape[1], pcs_target.shape[1]
        programs = scores.shape[1]
        width, slots = math.gcd(columns, WIDTH), 2
        if n_src == 4:
            width, slots = math.gcd(columns // n_src, WIDTH // 2), n_src
        pcs = pcs_source.shape[0]
        depth = depth_of(pcs)[1]
        f32, bf16 = jnp.float32, jnp.bfloat16
        sem = pltpu.SemaphoreType.DMA
        whole = pl.BlockSpec(memory_space=pltpu.VMEM)
        dense_r, dense_c = (rows // LANES, LANES), (columns // LANES, LANES)
        shapes = (
            pltpu.VMEM(dense_r, f32), pltpu.VMEM(dense_c, f32), pltpu.VMEM((columns, programs), f32)
        )
        results = pl.pallas_call(
            functools.partial(kernel, n_src, n_tgt),
            out_shape=shapes,
            in_specs=[whole] * 4,
            out_specs=(whole,) * 3,
            scratch_shapes=[
                pltpu.VMEM((2, rows, width), f32),
                pltpu.VMEM((slots, depth, rows), f32),
                pltpu.VMEM((depth, columns), f32),
                pltpu.VMEM((slots, rows, depth), bf16),
                pltpu.VMEM((depth, rows), bf16),
                pltpu.VMEM((columns, depth), bf16),
                pltpu.VMEM((depth, columns), bf16),
                pltpu.VMEM((slots, programs + 16, rows), bf16),
                pltpu.VMEM((2, rows, width), bf16),
                pltpu.VMEM((2, max(rows, columns) // LANES, 8, LANES), f32),
                pltpu.VMEM((columns // width, programs + 16, width), f32),
                pltpu.VMEM((columns // width, 8, width), f32),
                pltpu.VMEM((n_src, -(-(programs + pcs) // 32) * 32, rows), f32),
                pltpu.VMEM((ITERS, n_tgt) + dense_r, f32),
                pltpu.VMEM((ITERS, n_src) + dense_c, f32),
                pltpu.VMEM((n_src,) + dense_r, f32),
                pltpu.VMEM((n_src, -(-columns // n_src // (8 * LANES)) * 8, LANES), f32),
                sem((ITERS, 2, n_tgt)),
                sem((ITERS, 2, n_tgt)),
                sem((ITERS, 2, n_src)),
                sem((ITERS, 2, n_src)),
                sem((2, n_src, 3)),
                sem((2, n_src, 3)),
                sem((2, n_src, 3)),
                sem((2, n_src, 3)),
                sem((n_src,)),
                sem((n_src,)),
                sem((columns // width + 1, 2)),
                sem((columns // width + 1, 2)),
            ],
            compiler_params=pltpu.CompilerParams(
                collective_id=0, has_side_effects=True, vmem_limit_bytes=60 * 2**20
            ),
            name="coupling",
        )(pcs_source, pcs_target, growth.reshape(dense_r), scores)
        f, g, out = pl.pallas_call(
            deliver,
            out_shape=tuple(jax.ShapeDtypeStruct(shape.shape, f32) for shape in shapes),
            in_specs=[whole] * 3,
            out_specs=(pl.BlockSpec(memory_space=pl.ANY),) * 3,
            scratch_shapes=[sem((3,))],
            name="deliver",
        )(*[pltpu.with_memory_space_constraint(result, pltpu.VMEM) for result in results])
        return f.reshape(-1), g.reshape(-1), out

    in_specs = (P(None, "src"), P(None, "tgt"), P("src"), P("src", None))
    out_specs = (P("src"), P("tgt"), P("tgt", None))
    return jax.shard_map(shards, mesh=mesh, in_specs=in_specs, out_specs=out_specs, check_vma=False)
```

```python
import functools
import math

import jax
import jax.numpy as jnp
from jax import lax
from jax.experimental import pallas as pl
from jax.experimental.pallas import tpu as pltpu
from jax.sharding import PartitionSpec as P

ITERS = 2
EPSILON = 0.05
MARGIN = 1.0
FACTOR = MARGIN / (MARGIN + EPSILON)
LANES = 128
LOG2E = math.log2(math.e)
UNIT = EPSILON / LOG2E
MESH = pl.DeviceIdType.MESH
WIDTH, STEP, SUB = 512, 512, 64


def split3(value):
    high = value.astype(jnp.bfloat16).astype(jnp.float32)
    mid = (value - high).astype(jnp.bfloat16).astype(jnp.float32)
    return high, mid, value - high - mid


def depth_of(pcs):
    base = -(-pcs // 8) * 8
    return base, -(-(3 * base + 16) // LANES) * LANES


def augment(coords, wide_ref, scale, source):
    pcs, cells = coords.shape
    base, depth = depth_of(pcs)
    wide = coords.astype(jnp.float32)
    norm = -0.5 * scale * jnp.sum(wide * wide, axis=0, keepdims=True)
    at = lax.broadcasted_iota(jnp.int32, (16, cells), 0) - (0 if source else 3)
    high, mid, low = split3(norm)
    extra = jnp.where(at == 0, high, jnp.where(at == 1, mid, jnp.where(at == 2, low, 0.0)))
    at = lax.broadcasted_iota(jnp.int32, (16, cells), 0)
    ones = ((at >= 3) & (at < 6)) | ((at >= 11) & (at < 14)) if source else (at < 3) | ((at >= 8) & (at < 11))
    wide_ref[...] = jnp.zeros(wide_ref.shape, jnp.float32)
    for k, piece in enumerate(split3(scale * wide) if source else (wide,) * 3):
        wide_ref[k * base : k * base + pcs, :] = piece
    wide_ref[3 * base : 3 * base + 16, :] = jnp.where(ones, 1.0, extra)


def turn(wide_ref, rows_ref, first, last):
    depth = wide_ref.shape[0]
    for k in range(first // LANES, last // LANES):
        cut = slice(k * LANES, (k + 1) * LANES)
        for d in range(depth // LANES):
            deep = slice(d * LANES, (d + 1) * LANES)
            rows_ref[cut, deep] = wide_ref[deep, cut].T.astype(jnp.bfloat16)


def set_bias(dense, wide_ref, rows_ref, at, first):
    cells = dense.shape[0] * LANES
    for p, piece in enumerate(split3(dense)):
        for k in range(dense.shape[0]):
            lanes = slice(first + k * LANES, first + (k + 1) * LANES)
            wide_ref[at + p : at + p + 1, lanes] = piece[k : k + 1, :]
    turn(wide_ref, rows_ref, first, first + cells)


def halves_of(cells):
    parts = math.gcd(2, max(cells // (8 * LANES), 1))
    return [(p * (cells // parts), (p + 1) * (cells // parts)) for p in range(parts)]


def join(peak, total, block):
    t = block.reshape(-1, 8, LANES)
    newpeak = jnp.maximum(peak, jnp.max(t, axis=0))
    total = total * jnp.exp2(peak - newpeak) + jnp.sum(jnp.exp2(t - newpeak[None]), axis=0)
    return newpeak, total


def closed(peak, total):
    top = jnp.max(peak, axis=0, keepdims=True)
    return top, jnp.sum(total * jnp.exp2(peak - top), axis=0, keepdims=True)


def lse_pass(rows_ref, columns_ref, stats_ref, lse_ref, row_span, lane_span, fresh):
    (low, high), (begin, end) = row_span, lane_span
    width = math.gcd(end - begin, WIDTH)
    step = math.gcd(high - low, STEP)
    sub = math.gcd(step, SUB)
    halves = width // LANES

    def over_columns(c, unused):
        right = columns_ref[:, pl.ds(pl.multiple_of(begin + c * width, width), width)]
        tiles = [begin // LANES + c * halves + h for h in range(halves)]
        if fresh:
            empty = (jnp.full((8, LANES), -jnp.inf, jnp.float32), jnp.zeros((8, LANES), jnp.float32))
            stats = [empty] * halves
        else:
            stats = [(stats_ref[0, tile], stats_ref[1, tile]) for tile in tiles]
        for r in range((high - low) // step):
            block = jnp.dot(
                rows_ref[low + r * step : low + (r + 1) * step, :], right,
                preferred_element_type=jnp.float32,
            )
            for q in range(step // sub):
                for h in range(halves):
                    cut = block[q * sub : (q + 1) * sub, h * LANES : (h + 1) * LANES]
                    stats[h] = join(*stats[h], cut)
        for tile, (peak, total) in zip(tiles, stats):
            if lse_ref is None:
                stats_ref[0, tile] = peak
                stats_ref[1, tile] = total
            else:
                top, total = closed(peak, total)
                lse_ref[pl.ds(tile, 1), :] = top + jnp.log2(total)
        return unused

    lax.fori_loop(0, (end - begin) // width, over_columns, 0, unroll=True)


def fill_tile(rows_ref, right, tile_ref, row_span, peak):
    low, high = row_span
    width = tile_ref.shape[1]
    step = math.gcd(high - low, STEP)
    for r in range((high - low) // step):
        at = slice(low + r * step, low + (r + 1) * step)
        block = jnp.dot(rows_ref[at, :], right, preferred_element_type=jnp.float32)
        tile_ref[at, :] = block
        peak = jnp.maximum(peak, jnp.max(block.reshape(-1, 8, width), axis=0))
    return peak


def carry_tile(tile_ref, peak, scores_ref, weights):
    rows = tile_ref.shape[0]
    step = math.gcd(rows, STEP)
    for r in range(rows // step):
        at = slice(r * step, (r + 1) * step)
        weights[at, :] = jnp.exp2(tile_ref[at, :] - peak).astype(jnp.bfloat16)
    return jnp.dot(scores_ref[...], weights[...], preferred_element_type=jnp.float32)


def kernel(
    n_src, n_tgt, xs_ref, yt_ref, growth_ref, scores_far, f_ref, g_ref, out_ref,
    scores_ref, scores_sem, tile, x_wide, y_wide, x_rows, x_cols, y_rows, y_cols, scores_t, weights, running, sums, peaks, pay,
    row_buf, col_buf, f_all, g_all, row_send, row_recv, col_send, col_recv,
    bulk_send, bulk_recv, pass_send, pass_recv, f_send, f_recv, out_send, out_recv,
):
    fetch = pltpu.make_async_copy(scores_far, scores_ref, scores_sem)
    fetch.start()
    src, tgt = lax.axis_index("src"), lax.axis_index("tgt")
    barrier = pltpu.get_barrier_semaphore()
    for k in range(1, n_src):
        pl.semaphore_signal(
            barrier, inc=1, device_id={"src": lax.rem(src + k, n_src)}, device_id_type=MESH
        )
    for k in range(1, n_tgt):
        pl.semaphore_signal(
            barrier, inc=1, device_id={"tgt": lax.rem(tgt + k, n_tgt)}, device_id_type=MESH
        )

    pcs, rows = xs_ref.shape
    columns = yt_ref.shape[1]
    programs = scores_ref.shape[1]
    scale = 2.0 * LOG2E / (pcs * EPSILON)
    bias_at = 3 * depth_of(pcs)[0] + 8
    augment(yt_ref[...], y_wide, scale, False)
    y_cols[...] = y_wide[...].astype(jnp.bfloat16)
    turn(y_wide, y_rows, 0, columns)
    augment(xs_ref[...], x_wide.at[0], scale, True)
    x_cols[...] = x_wide[0].astype(jnp.bfloat16)

    pay[0, programs:, :] = jnp.zeros((pay.shape[1] - programs, rows), jnp.float32)
    pay[0, programs : programs + pcs, :] = xs_ref[...].astype(jnp.float32)
    fetch.wait()
    for k in range(rows // LANES):
        cut = slice(k * LANES, (k + 1) * LANES)
        pay[0, 0:programs, cut] = scores_ref[cut, :].astype(jnp.float32).T
    scores_t[0, 0:programs, :] = pay[0, 0:programs, :].astype(jnp.bfloat16)
    for p in range(scores_t.shape[0]):
        scores_t[p, programs:, :] = jnp.ones((16, rows), jnp.bfloat16)

    bits = [1 << b for b in range(n_src.bit_length() - 1)]
    core, share = lax.rem(tgt, 2), pay.shape[1] // 4

    def relative(mask):
        there = src
        for bit in bits:
            if mask & bit:
                there = there + bit - 2 * bit * lax.rem(lax.div(src, bit), 2)
        return there

    early = max(share // 5 // 8 * 8, 8)
    marks = [0, early, max(share - early, early), share]
    spans_of_share = list(zip(marks, marks[1:]))
    parts = range(len(spans_of_share))

    def lines_at(order, part):
        low, high = spans_of_share[part]
        return pl.ds(pl.multiple_of((2 * core + order) * share + low, 8), high - low)

    bulk, passed = {}, {}

    def ship(order, bit, mask, part):
        lines, there = lines_at(order, part), mask ^ bit
        copy = pltpu.make_async_remote_copy(
            src_ref=pay.at[mask, lines], dst_ref=pay.at[there, lines],
            send_sem=bulk_send.at[order, there, part], recv_sem=bulk_recv.at[order, there, part],
            device_id={"src": relative(bit)}, device_id_type=MESH,
        )
        copy.start()
        bulk[order, there, part] = copy

    def hand_over(mask, chosen=(0, 1), pieces=parts):
        for part in pieces:
            for order in chosen:
                if (order, mask, part) in passed:
                    continue
                bulk[order, mask, part].wait_recv()
                lines = lines_at(order, part)
                copy = pltpu.make_async_remote_copy(
                    src_ref=pay.at[mask, lines], dst_ref=pay.at[mask, lines],
                    send_sem=pass_send.at[order, mask, part],
                    recv_sem=pass_recv.at[order, mask, part],
                    device_id={"tgt": tgt + 1 - 2 * core}, device_id_type=MESH,
                )
                copy.start()
                passed[order, mask, part] = copy

    orders = [bits, bits[::-1]]

    def ship_own(stages, chosen):
        for t in stages:
            for part in chosen:
                for order, bit in enumerate(orders):
                    ship(order, bit[t], 0, part)

    def ship_rest(chosen):
        for order, bit in enumerate(orders):
            hand_over(bit[0], (order,))
        for t in range(1, len(bits)):
            for order, bit in enumerate(orders):
                held = [0]
                for b in bit[:t]:
                    held += [m ^ b for m in held]
                for mask in held[1:]:
                    hand_over(mask, (order,))
                    for part in chosen:
                        ship(order, bit[t], mask, part)

    def exchange(buf, axis, me, n, send, recv, lines):
        copies = [
            pltpu.make_async_remote_copy(
                src_ref=buf.at[me, lines], dst_ref=buf.at[me, lines],
                send_sem=send.at[k], recv_sem=recv.at[k],
                device_id={axis: lax.rem(me + k, n)}, device_id_type=MESH,
            )
            for k in range(1, n)
        ]
        for copy in copies:
            copy.start()
        return copies

    def joined(buf, n, lines):
        parts = [buf[d, lines] for d in range(n)]
        top = functools.reduce(jnp.maximum, parts)
        return top + jnp.log2(sum(jnp.exp2(part - top) for part in parts))

    log_a = jnp.log2(growth_ref[...]) - math.log2(rows * n_src)
    log_b = -math.log2(columns * n_tgt)
    quarters = n_src == 4
    source_halves, target_halves = halves_of(rows), halves_of(columns)

    def lines_of(span):
        return slice(span[0] // LANES, span[1] // LANES)

    def finish(rows_ref, columns_ref, row_span, spans, fresh, buf, axis, me, n, send, recv):
        sent = []
        for h, span in enumerate(spans):
            lse_pass(rows_ref, columns_ref, running, buf.at[me], row_span, span, fresh)
            sent.append(exchange(buf, axis, me, n, send.at[h], recv.at[h], lines_of(span)))
        return sent

    def settle(copies):
        for copy in copies:
            copy.wait()

    for step in range(ITERS):
        over_tgt = (row_buf.at[step], "tgt", tgt, n_tgt, row_send.at[step], row_recv.at[step])
        over_src = (col_buf.at[step], "src", src, n_src, col_send.at[step], col_recv.at[step])
        if step == 0:
            pl.semaphore_wait(barrier, n_src + n_tgt - 2)
            ship_own(range(1), parts)
            ship_own(range(1, len(bits)), parts[:1])
            sent = finish(y_rows, x_cols, (0, columns), source_halves, True, *over_tgt)
        else:
            for h, span in enumerate(target_halves):
                settle(sent[h])
                lines = lines_of(span)
                g = FACTOR * (log_b - joined(col_buf.at[step - 1], n_src, lines))
                set_bias(g, y_wide, y_rows, bias_at + 3, span[0])
                if h < len(target_halves) - 1:
                    lse_pass(y_rows, x_cols, running, None, span, (0, rows), h == 0)
            sent = finish(y_rows, x_cols, span, source_halves, h == 0, *over_tgt)
        if step == ITERS - 1:
            break
        for h, span in enumerate(source_halves):
            settle(sent[h])
            lines = lines_of(span)
            f = FACTOR * (log_a[lines] - joined(row_buf.at[step], n_tgt, lines))
            set_bias(f, x_wide.at[0], x_rows.at[0], bias_at, span[0])
            if h < len(source_halves) - 1:
                lse_pass(x_rows.at[0], y_cols, running, None, span, (0, columns), h == 0)
        sent = finish(x_rows.at[0], y_cols, span, target_halves, h == 0, *over_src)
        if step == 0:
            ship_own(range(1, len(bits)), parts[1:])
            if quarters:
                ship_rest(parts[:-1])

    width, slots = tile.shape[2], x_rows.shape[0]
    groups, halves = columns // width, width // LANES
    piece = columns // n_src
    empty = jnp.full((8, width), -jnp.inf, jnp.float32)

    def fill(block, start, slot, span, peak):
        right = y_cols[:, pl.ds(pl.multiple_of(start, width), width)]
        return fill_tile(x_rows.at[block % slots], right, tile.at[slot], span, peak)

    def unpack(block):
        hand_over(block)
        for order in range(2):
            for part in parts:
                passed[order, block, part].wait_recv()
        augment(pay[block, programs : programs + pcs, :], x_wide.at[block % slots], scale, True)
        scores_t[block % slots, 0:programs, :] = pay[block, 0:programs, :].astype(jnp.bfloat16)

    def admit(block):
        shared[block].wait_recv()
        slot = block % slots
        set_bias(f_all[block], x_wide.at[slot], x_rows.at[slot], bias_at, 0)

    def carry(block, start, place, slot, ready):
        peak = jnp.max(ready, axis=0, keepdims=True)
        if block > 0:
            before = peaks[place, 0:1, :]
            peak = jnp.maximum(peak, before)
        carried = carry_tile(tile.at[slot], peak, scores_t.at[block % slots], weights.at[slot])
        if block > 0:
            carried = carried + sums[place] * jnp.exp2(before - peak)
        if block < n_src - 1:
            sums[place] = carried
            peaks[place, 0:1, :] = peak
            return
        mass = carried[programs : programs + 1, :]
        g = UNIT * FACTOR * (log_b - (peak + jnp.log2(mass)))
        carried = carried[0:programs, :] / mass
        for h in range(halves):
            cut = slice(h * LANES, (h + 1) * LANES)
            at = start + h * LANES
            owner = lax.div(at, piece)
            g_all[owner, pl.ds(lax.div(at - owner * piece, LANES), 1), :] = g[:, cut]
            out_ref[pl.ds(pl.multiple_of(at, LANES), LANES), :] = carried[:, cut].T

    if quarters:
        for block in range(1, n_src - 1):
            hand_over(block)
        for block in range(1, n_src - 1):
            unpack(block)
    ready, shared = empty, {}
    for h, span in enumerate(source_halves):
        settle(sent[h])
        lines = lines_of(span)
        f = FACTOR * (log_a[lines] - joined(row_buf.at[ITERS - 1], n_tgt, lines))
        f_ref[lines, :] = UNIT * f
        f_all[0, lines, :] = f
        if h == len(source_halves) - 1:
            for mask in range(1, n_src):
                shared[mask] = pltpu.make_async_remote_copy(
                    src_ref=f_all.at[0], dst_ref=f_all.at[mask],
                    send_sem=f_send.at[mask], recv_sem=f_recv.at[mask],
                    device_id={"src": relative(mask)}, device_id_type=MESH,
                )
                shared[mask].start()
            ship_rest(parts[-1:] if quarters else parts)
        set_bias(f, x_wide.at[0], x_rows.at[0], bias_at, span[0])
        if quarters:
            ready = fill(0, src * piece, 0, span, ready)

    gathered = []
    if quarters:
        wide = piece // width
        mine = [(src * piece + c * width, c) for c in range(wide)]
        spare = [((3 - src) * piece + c * width, wide + c) for c in range(wide)]
        order = [(0, spot) for spot in mine + spare]
        order += [(block, spot) for spot in mine + spare for block in range(1, n_src)]
        for u, (block, spot) in enumerate(order):
            now, after = ready, order[u + 1] if u + 1 < len(order) else None
            fresh = after and after[0] > block and after[1][1] == 0
            if fresh and after[0] == 1:
                carry(block, *spot, u % 2, now)
                now = None
                hand_over(n_src - 1, pieces=parts[:-1])
            if fresh:
                if after[0] == n_src - 2:
                    hand_over(n_src - 1)
                if after[0] == n_src - 1:
                    unpack(after[0])
                admit(after[0])
            if after:
                ready = fill(after[0], after[1][0], (u + 1) % 2, (0, rows), empty)
            if now is not None:
                carry(block, *spot, u % 2, now)
            if block == n_src - 1 and spot[1] < wide:
                at = pl.ds(pl.multiple_of(spot[0], width), width)
                refs = [out_ref.at[at, :]] + [g_all.at[src]] * (spot[1] == wide - 1)
                for k, bit in enumerate(bits):
                    for slot, ref in enumerate(refs):
                        where = spot[1] if slot == 0 else wide
                        copy = pltpu.make_async_remote_copy(
                            src_ref=ref, dst_ref=ref,
                            send_sem=out_send.at[where, k], recv_sem=out_recv.at[where, k],
                            device_id={"src": relative(bit)}, device_id_type=MESH,
                        )
                        copy.start()
                        gathered.append(copy)
    else:
        for block in range(n_src):
            if block > 0:
                unpack(block)
                admit(block)

            def over_groups(c, unused, block=block):
                start = c * width
                carry(block, start, c, 0, fill(block, start, 0, (0, rows), empty))
                return unused

            lax.fori_loop(0, groups, over_groups, 0)
    for copy in gathered:
        copy.wait()
    for k in range(n_src):
        g_ref[k * (piece // LANES) : (k + 1) * (piece // LANES), :] = g_all[k, 0 : piece // LANES, :]
    for copy in [*bulk.values(), *passed.values(), *shared.values()]:
        copy.wait_send()


def deliver(f_ref, g_ref, out_ref, f_end, g_end, out_end, sems):
    refs = ((f_ref, f_end), (g_ref, g_end), (out_ref, out_end))
    copies = [pltpu.make_async_copy(a, b, sems.at[k]) for k, (a, b) in enumerate(refs)]
    for copy in copies:
        copy.start()
    for copy in copies:
        copy.wait()


def solution(mesh):
    n_src, n_tgt = mesh.shape["src"], mesh.shape["tgt"]

    def shards(pcs_source, pcs_target, growth, scores):
        rows, columns = pcs_source.shape[1], pcs_target.shape[1]
        programs = scores.shape[1]
        width, slots = math.gcd(columns, WIDTH), 2
        if n_src == 4:
            width, slots = math.gcd(columns // n_src, WIDTH // 2), n_src
        pcs = pcs_source.shape[0]
        depth = depth_of(pcs)[1]
        f32, bf16 = jnp.float32, jnp.bfloat16
        sem = pltpu.SemaphoreType.DMA
        whole = pl.BlockSpec(memory_space=pltpu.VMEM)
        dense_r, dense_c = (rows // LANES, LANES), (columns // LANES, LANES)
        shapes = (
            pltpu.VMEM(dense_r, f32), pltpu.VMEM(dense_c, f32), pltpu.VMEM((columns, programs), f32)
        )
        results = pl.pallas_call(
            functools.partial(kernel, n_src, n_tgt),
            out_shape=shapes,
            in_specs=[whole] * 3 + [pl.BlockSpec(memory_space=pl.ANY)],
            out_specs=(whole,) * 3,
            scratch_shapes=[
                pltpu.VMEM((rows, programs), bf16),
                sem(()),
                pltpu.VMEM((2, rows, width), f32),
                pltpu.VMEM((slots, depth, rows), f32),
                pltpu.VMEM((depth, columns), f32),
                pltpu.VMEM((slots, rows, depth), bf16),
                pltpu.VMEM((depth, rows), bf16),
                pltpu.VMEM((columns, depth), bf16),
                pltpu.VMEM((depth, columns), bf16),
                pltpu.VMEM((slots, programs + 16, rows), bf16),
                pltpu.VMEM((2, rows, width), bf16),
                pltpu.VMEM((2, max(rows, columns) // LANES, 8, LANES), f32),
                pltpu.VMEM((columns // width, programs + 16, width), f32),
                pltpu.VMEM((columns // width, 8, width), f32),
                pltpu.VMEM((n_src, -(-(programs + pcs) // 32) * 32, rows), f32),
                pltpu.VMEM((ITERS, n_tgt) + dense_r, f32),
                pltpu.VMEM((ITERS, n_src) + dense_c, f32),
                pltpu.VMEM((n_src,) + dense_r, f32),
                pltpu.VMEM((n_src, -(-columns // n_src // (8 * LANES)) * 8, LANES), f32),
                sem((ITERS, 2, n_tgt)),
                sem((ITERS, 2, n_tgt)),
                sem((ITERS, 2, n_src)),
                sem((ITERS, 2, n_src)),
                sem((2, n_src, 3)),
                sem((2, n_src, 3)),
                sem((2, n_src, 3)),
                sem((2, n_src, 3)),
                sem((n_src,)),
                sem((n_src,)),
                sem((columns // width + 1, 2)),
                sem((columns // width + 1, 2)),
            ],
            compiler_params=pltpu.CompilerParams(
                collective_id=0, has_side_effects=True, vmem_limit_bytes=60 * 2**20
            ),
            name="coupling",
        )(pcs_source, pcs_target, growth.reshape(dense_r), scores)
        f, g, out = pl.pallas_call(
            deliver,
            out_shape=tuple(jax.ShapeDtypeStruct(shape.shape, f32) for shape in shapes),
            in_specs=[whole] * 3,
            out_specs=(pl.BlockSpec(memory_space=pl.ANY),) * 3,
            scratch_shapes=[sem((3,))],
            name="deliver",
        )(*[pltpu.with_memory_space_constraint(result, pltpu.VMEM) for result in results])
        return f.reshape(-1), g.reshape(-1), out

    in_specs = (P(None, "src"), P(None, "tgt"), P("src"), P("src", None))
    out_specs = (P("src"), P("tgt"), P("tgt", None))
    return jax.shard_map(shards, mesh=mesh, in_specs=in_specs, out_specs=out_specs, check_vma=False)
```

```python
import functools
import math

import jax
import jax.numpy as jnp
from jax import lax
from jax.experimental import pallas as pl
from jax.experimental.pallas import tpu as pltpu
from jax.sharding import PartitionSpec as P

ITERS = 2
EPSILON = 0.05
MARGIN = 1.0
FACTOR = MARGIN / (MARGIN + EPSILON)
LANES = 128
LOG2E = math.log2(math.e)
UNIT = EPSILON / LOG2E
MESH = pl.DeviceIdType.MESH
WIDTH, STEP, SUB = 512, 512, 64


def split3(value):
    high = value.astype(jnp.bfloat16).astype(jnp.float32)
    mid = (value - high).astype(jnp.bfloat16).astype(jnp.float32)
    return high, mid, value - high - mid


def depth_of(pcs):
    base = -(-pcs // 8) * 8
    return base, -(-(3 * base + 16) // LANES) * LANES


def augment(coords, wide_ref, scale, source):
    pcs, cells = coords.shape
    base, depth = depth_of(pcs)
    wide = coords.astype(jnp.float32)
    norm = -0.5 * scale * jnp.sum(wide * wide, axis=0, keepdims=True)
    at = lax.broadcasted_iota(jnp.int32, (16, cells), 0) - (0 if source else 3)
    high, mid, low = split3(norm)
    extra = jnp.where(at == 0, high, jnp.where(at == 1, mid, jnp.where(at == 2, low, 0.0)))
    at = lax.broadcasted_iota(jnp.int32, (16, cells), 0)
    ones = ((at >= 3) & (at < 6)) | ((at >= 11) & (at < 14)) if source else (at < 3) | ((at >= 8) & (at < 11))
    wide_ref[...] = jnp.zeros(wide_ref.shape, jnp.float32)
    for k, piece in enumerate(split3(scale * wide) if source else (wide,) * 3):
        wide_ref[k * base : k * base + pcs, :] = piece
    wide_ref[3 * base : 3 * base + 16, :] = jnp.where(ones, 1.0, extra)


def turn(wide_ref, rows_ref, first, last):
    depth = wide_ref.shape[0]
    for k in range(first // LANES, last // LANES):
        cut = slice(k * LANES, (k + 1) * LANES)
        for d in range(depth // LANES):
            deep = slice(d * LANES, (d + 1) * LANES)
            rows_ref[cut, deep] = wide_ref[deep, cut].T.astype(jnp.bfloat16)


def set_bias(dense, wide_ref, rows_ref, at, first):
    cells = dense.shape[0] * LANES
    for p, piece in enumerate(split3(dense)):
        for k in range(dense.shape[0]):
            lanes = slice(first + k * LANES, first + (k + 1) * LANES)
            wide_ref[at + p : at + p + 1, lanes] = piece[k : k + 1, :]
    turn(wide_ref, rows_ref, first, first + cells)


def halves_of(cells):
    parts = math.gcd(2, max(cells // (8 * LANES), 1))
    return [(p * (cells // parts), (p + 1) * (cells // parts)) for p in range(parts)]


def join(peak, total, block):
    t = block.reshape(-1, 8, LANES)
    newpeak = jnp.maximum(peak, jnp.max(t, axis=0))
    total = total * jnp.exp2(peak - newpeak) + jnp.sum(jnp.exp2(t - newpeak[None]), axis=0)
    return newpeak, total


def closed(peak, total):
    top = jnp.max(peak, axis=0, keepdims=True)
    return top, jnp.sum(total * jnp.exp2(peak - top), axis=0, keepdims=True)


def lse_pass(rows_ref, columns_ref, stats_ref, lse_ref, row_span, lane_span, fresh):
    (low, high), (begin, end) = row_span, lane_span
    width = math.gcd(end - begin, WIDTH)
    step = math.gcd(high - low, STEP)
    sub = math.gcd(step, SUB)
    halves = width // LANES

    def over_columns(c, unused):
        right = columns_ref[:, pl.ds(pl.multiple_of(begin + c * width, width), width)]
        tiles = [begin // LANES + c * halves + h for h in range(halves)]
        if fresh:
            empty = (jnp.full((8, LANES), -jnp.inf, jnp.float32), jnp.zeros((8, LANES), jnp.float32))
            stats = [empty] * halves
        else:
            stats = [(stats_ref[0, tile], stats_ref[1, tile]) for tile in tiles]
        for r in range((high - low) // step):
            block = jnp.dot(
                rows_ref[low + r * step : low + (r + 1) * step, :], right,
                preferred_element_type=jnp.float32,
            )
            for q in range(step // sub):
                for h in range(halves):
                    cut = block[q * sub : (q + 1) * sub, h * LANES : (h + 1) * LANES]
                    stats[h] = join(*stats[h], cut)
        for tile, (peak, total) in zip(tiles, stats):
            if lse_ref is None:
                stats_ref[0, tile] = peak
                stats_ref[1, tile] = total
            else:
                top, total = closed(peak, total)
                lse_ref[pl.ds(tile, 1), :] = top + jnp.log2(total)
        return unused

    lax.fori_loop(0, (end - begin) // width, over_columns, 0, unroll=True)


def fill_tile(rows_ref, right, tile_ref, row_span, peak):
    low, high = row_span
    width = tile_ref.shape[1]
    step = math.gcd(high - low, STEP)
    for r in range((high - low) // step):
        at = slice(low + r * step, low + (r + 1) * step)
        block = jnp.dot(rows_ref[at, :], right, preferred_element_type=jnp.float32)
        tile_ref[at, :] = block
        peak = jnp.maximum(peak, jnp.max(block.reshape(-1, 8, width), axis=0))
    return peak


def carry_tile(tile_ref, peak, scores_ref, weights):
    rows = tile_ref.shape[0]
    step = math.gcd(rows, STEP)
    for r in range(rows // step):
        at = slice(r * step, (r + 1) * step)
        weights[at, :] = jnp.exp2(tile_ref[at, :] - peak).astype(jnp.bfloat16)
    return jnp.dot(scores_ref[...], weights[...], preferred_element_type=jnp.float32)


def kernel(
    n_src, n_tgt, xs_ref, yt_ref, growth_ref, scores_far, f_ref, g_ref, out_ref,
    scores_ref, scores_sem, tile, x_wide, y_wide, x_rows, x_cols, y_rows, y_cols, scores_t, weights, running, sums, peaks, pay,
    row_buf, col_buf, f_all, g_all, row_send, row_recv, col_send, col_recv,
    bulk_send, bulk_recv, pass_send, pass_recv, f_send, f_recv, out_send, out_recv,
):
    fetch = pltpu.make_async_copy(scores_far, scores_ref, scores_sem)
    fetch.start()
    src, tgt = lax.axis_index("src"), lax.axis_index("tgt")
    barrier = pltpu.get_barrier_semaphore()
    for k in range(1, n_src):
        pl.semaphore_signal(
            barrier, inc=1, device_id={"src": lax.rem(src + k, n_src)}, device_id_type=MESH
        )
    for k in range(1, n_tgt):
        pl.semaphore_signal(
            barrier, inc=1, device_id={"tgt": lax.rem(tgt + k, n_tgt)}, device_id_type=MESH
        )

    pcs, rows = xs_ref.shape
    columns = yt_ref.shape[1]
    programs = scores_ref.shape[1]
    scale = 2.0 * LOG2E / (pcs * EPSILON)
    bias_at = 3 * depth_of(pcs)[0] + 8
    augment(yt_ref[...], y_wide, scale, False)
    y_cols[...] = y_wide[...].astype(jnp.bfloat16)
    turn(y_wide, y_rows, 0, columns)
    augment(xs_ref[...], x_wide.at[0], scale, True)
    x_cols[...] = x_wide[0].astype(jnp.bfloat16)

    pay[0, programs:, :] = jnp.zeros((pay.shape[1] - programs, rows), jnp.float32)
    pay[0, programs : programs + pcs, :] = xs_ref[...].astype(jnp.float32)
    fetch.wait()
    for k in range(rows // LANES):
        cut = slice(k * LANES, (k + 1) * LANES)
        pay[0, 0:programs, cut] = scores_ref[cut, :].astype(jnp.float32).T
    scores_t[0, 0:programs, :] = pay[0, 0:programs, :].astype(jnp.bfloat16)
    for p in range(scores_t.shape[0]):
        scores_t[p, programs:, :] = jnp.ones((16, rows), jnp.bfloat16)

    bits = [1 << b for b in range(n_src.bit_length() - 1)]
    core, share = lax.rem(tgt, 2), pay.shape[1] // 4

    def across(me, mask):
        there = me
        for b in range(mask.bit_length()):
            if mask >> b & 1:
                there = there + (1 << b) - (2 << b) * lax.rem(lax.div(me, 1 << b), 2)
        return there

    def relative(mask):
        return across(src, mask)

    early = max(share // 5 // 8 * 8, 8)
    marks = [0, early, max(share - early, early), share]
    spans_of_share = list(zip(marks, marks[1:]))
    parts = range(len(spans_of_share))

    def lines_at(order, part):
        low, high = spans_of_share[part]
        return pl.ds(pl.multiple_of((2 * core + order) * share + low, 8), high - low)

    bulk, passed = {}, {}

    def ship(order, bit, mask, part):
        lines, there = lines_at(order, part), mask ^ bit
        copy = pltpu.make_async_remote_copy(
            src_ref=pay.at[mask, lines], dst_ref=pay.at[there, lines],
            send_sem=bulk_send.at[order, there, part], recv_sem=bulk_recv.at[order, there, part],
            device_id={"src": relative(bit)}, device_id_type=MESH,
        )
        copy.start()
        bulk[order, there, part] = copy

    def hand_over(mask, chosen=(0, 1), pieces=parts):
        for part in pieces:
            for order in chosen:
                if (order, mask, part) in passed:
                    continue
                bulk[order, mask, part].wait_recv()
                lines = lines_at(order, part)
                copy = pltpu.make_async_remote_copy(
                    src_ref=pay.at[mask, lines], dst_ref=pay.at[mask, lines],
                    send_sem=pass_send.at[order, mask, part],
                    recv_sem=pass_recv.at[order, mask, part],
                    device_id={"tgt": tgt + 1 - 2 * core}, device_id_type=MESH,
                )
                copy.start()
                passed[order, mask, part] = copy

    orders = [bits, bits[::-1]]

    def ship_own(stages, chosen):
        for t in stages:
            for part in chosen:
                for order, bit in enumerate(orders):
                    ship(order, bit[t], 0, part)

    def ship_rest(chosen):
        for order, bit in enumerate(orders):
            hand_over(bit[0], (order,))
        for t in range(1, len(bits)):
            for order, bit in enumerate(orders):
                held = [0]
                for b in bit[:t]:
                    held += [m ^ b for m in held]
                for mask in held[1:]:
                    hand_over(mask, (order,))
                    for part in chosen:
                        ship(order, bit[t], mask, part)

    def exchange(buf, axis, me, n, send, recv, lines):
        copies = [
            pltpu.make_async_remote_copy(
                src_ref=buf.at[me, lines], dst_ref=buf.at[me, lines],
                send_sem=send.at[k], recv_sem=recv.at[k],
                device_id={axis: across(me, k)}, device_id_type=MESH,
            )
            for k in range(n - 1, 0, -1)
        ]
        for copy in copies:
            copy.start()
        return copies

    def joined(buf, n, lines):
        parts = [buf[d, lines] for d in range(n)]
        top = functools.reduce(jnp.maximum, parts)
        return top + jnp.log2(sum(jnp.exp2(part - top) for part in parts))

    log_a = jnp.log2(growth_ref[...]) - math.log2(rows * n_src)
    log_b = -math.log2(columns * n_tgt)
    quarters = n_src == 4
    source_halves, target_halves = halves_of(rows), halves_of(columns)

    def lines_of(span):
        return slice(span[0] // LANES, span[1] // LANES)

    def finish(rows_ref, columns_ref, row_span, spans, fresh, buf, axis, me, n, send, recv):
        sent = []
        for h, span in enumerate(spans):
            lse_pass(rows_ref, columns_ref, running, buf.at[me], row_span, span, fresh)
            sent.append(exchange(buf, axis, me, n, send.at[h], recv.at[h], lines_of(span)))
        return sent

    def settle(copies):
        for copy in copies:
            copy.wait()

    for step in range(ITERS):
        over_tgt = (row_buf.at[step], "tgt", tgt, n_tgt, row_send.at[step], row_recv.at[step])
        over_src = (col_buf.at[step], "src", src, n_src, col_send.at[step], col_recv.at[step])
        if step == 0:
            pl.semaphore_wait(barrier, n_src + n_tgt - 2)
            ship_own(range(1), parts)
            ship_own(range(1, len(bits)), parts[:1])
            sent = finish(y_rows, x_cols, (0, columns), source_halves, True, *over_tgt)
        else:
            for h, span in enumerate(target_halves):
                settle(sent[h])
                lines = lines_of(span)
                g = FACTOR * (log_b - joined(col_buf.at[step - 1], n_src, lines))
                set_bias(g, y_wide, y_rows, bias_at + 3, span[0])
                if h < len(target_halves) - 1:
                    lse_pass(y_rows, x_cols, running, None, span, (0, rows), h == 0)
            sent = finish(y_rows, x_cols, span, source_halves, h == 0, *over_tgt)
        if step == ITERS - 1:
            break
        for h, span in enumerate(source_halves):
            settle(sent[h])
            lines = lines_of(span)
            f = FACTOR * (log_a[lines] - joined(row_buf.at[step], n_tgt, lines))
            set_bias(f, x_wide.at[0], x_rows.at[0], bias_at, span[0])
            if h < len(source_halves) - 1:
                lse_pass(x_rows.at[0], y_cols, running, None, span, (0, columns), h == 0)
        sent = finish(x_rows.at[0], y_cols, span, target_halves, h == 0, *over_src)
        if step == 0:
            ship_own(range(1, len(bits)), parts[1:])
            if quarters:
                ship_rest(parts[:-1])

    width, slots = tile.shape[2], x_rows.shape[0]
    groups, halves = columns // width, width // LANES
    piece = columns // n_src
    empty = jnp.full((8, width), -jnp.inf, jnp.float32)

    def fill(block, start, slot, span, peak):
        right = y_cols[:, pl.ds(pl.multiple_of(start, width), width)]
        return fill_tile(x_rows.at[block % slots], right, tile.at[slot], span, peak)

    def unpack(block):
        hand_over(block)
        for order in range(2):
            for part in parts:
                passed[order, block, part].wait_recv()
        augment(pay[block, programs : programs + pcs, :], x_wide.at[block % slots], scale, True)
        scores_t[block % slots, 0:programs, :] = pay[block, 0:programs, :].astype(jnp.bfloat16)

    def admit(block):
        shared[block].wait_recv()
        slot = block % slots
        set_bias(f_all[block], x_wide.at[slot], x_rows.at[slot], bias_at, 0)

    def carry(block, start, place, slot, ready):
        peak = jnp.max(ready, axis=0, keepdims=True)
        if block > 0:
            before = peaks[place, 0:1, :]
            peak = jnp.maximum(peak, before)
        carried = carry_tile(tile.at[slot], peak, scores_t.at[block % slots], weights.at[slot])
        if block > 0:
            carried = carried + sums[place] * jnp.exp2(before - peak)
        if block < n_src - 1:
            sums[place] = carried
            peaks[place, 0:1, :] = peak
            return
        mass = carried[programs : programs + 1, :]
        g = UNIT * FACTOR * (log_b - (peak + jnp.log2(mass)))
        carried = carried[0:programs, :] / mass
        for h in range(halves):
            cut = slice(h * LANES, (h + 1) * LANES)
            at = start + h * LANES
            owner = lax.div(at, piece)
            g_all[owner, pl.ds(lax.div(at - owner * piece, LANES), 1), :] = g[:, cut]
            out_ref[pl.ds(pl.multiple_of(at, LANES), LANES), :] = carried[:, cut].T

    if quarters:
        for block in range(1, n_src - 1):
            hand_over(block)
        for block in range(1, n_src - 1):
            unpack(block)
    ready, shared = empty, {}
    for h, span in enumerate(source_halves):
        settle(sent[h])
        lines = lines_of(span)
        f = FACTOR * (log_a[lines] - joined(row_buf.at[ITERS - 1], n_tgt, lines))
        f_ref[lines, :] = UNIT * f
        f_all[0, lines, :] = f
        if h == len(source_halves) - 1:
            for mask in range(1, n_src):
                shared[mask] = pltpu.make_async_remote_copy(
                    src_ref=f_all.at[0], dst_ref=f_all.at[mask],
                    send_sem=f_send.at[mask], recv_sem=f_recv.at[mask],
                    device_id={"src": relative(mask)}, device_id_type=MESH,
                )
                shared[mask].start()
            ship_rest(parts[-1:] if quarters else parts)
        set_bias(f, x_wide.at[0], x_rows.at[0], bias_at, span[0])
        if quarters:
            ready = fill(0, src * piece, 0, span, ready)

    gathered = []
    if quarters:
        wide = piece // width
        mine = [(src * piece + c * width, c) for c in range(wide)]
        spare = [((3 - src) * piece + c * width, wide + c) for c in range(wide)]
        order = [(0, spot) for spot in mine + spare]
        order += [(block, spot) for spot in mine + spare for block in range(1, n_src)]
        for u, (block, spot) in enumerate(order):
            now, after = ready, order[u + 1] if u + 1 < len(order) else None
            fresh = after and after[0] > block and after[1][1] == 0
            if fresh and after[0] == 1:
                carry(block, *spot, u % 2, now)
                now = None
                hand_over(n_src - 1, pieces=parts[:-1])
            if fresh:
                if after[0] == n_src - 2:
                    hand_over(n_src - 1)
                if after[0] == n_src - 1:
                    unpack(after[0])
                admit(after[0])
            if after:
                ready = fill(after[0], after[1][0], (u + 1) % 2, (0, rows), empty)
            if now is not None:
                carry(block, *spot, u % 2, now)
            if block == n_src - 1 and spot[1] < wide:
                at = pl.ds(pl.multiple_of(spot[0], width), width)
                refs = [out_ref.at[at, :]] + [g_all.at[src]] * (spot[1] == wide - 1)
                for k, bit in enumerate(bits):
                    for slot, ref in enumerate(refs):
                        where = spot[1] if slot == 0 else wide
                        copy = pltpu.make_async_remote_copy(
                            src_ref=ref, dst_ref=ref,
                            send_sem=out_send.at[where, k], recv_sem=out_recv.at[where, k],
                            device_id={"src": relative(bit)}, device_id_type=MESH,
                        )
                        copy.start()
                        gathered.append(copy)
    else:
        for block in range(n_src):
            if block > 0:
                unpack(block)
                admit(block)

            def over_groups(c, unused, block=block):
                start = c * width
                carry(block, start, c, 0, fill(block, start, 0, (0, rows), empty))
                return unused

            lax.fori_loop(0, groups, over_groups, 0)
    for copy in gathered:
        copy.wait()
    for k in range(n_src):
        g_ref[k * (piece // LANES) : (k + 1) * (piece // LANES), :] = g_all[k, 0 : piece // LANES, :]
    for copy in [*bulk.values(), *passed.values(), *shared.values()]:
        copy.wait_send()


def deliver(f_ref, g_ref, out_ref, f_end, g_end, out_end, sems):
    refs = ((f_ref, f_end), (g_ref, g_end), (out_ref, out_end))
    copies = [pltpu.make_async_copy(a, b, sems.at[k]) for k, (a, b) in enumerate(refs)]
    for copy in copies:
        copy.start()
    for copy in copies:
        copy.wait()


def solution(mesh):
    n_src, n_tgt = mesh.shape["src"], mesh.shape["tgt"]

    def shards(pcs_source, pcs_target, growth, scores):
        rows, columns = pcs_source.shape[1], pcs_target.shape[1]
        programs = scores.shape[1]
        width, slots = math.gcd(columns, WIDTH), 2
        if n_src == 4:
            width, slots = math.gcd(columns // n_src, WIDTH // 2), n_src
        pcs = pcs_source.shape[0]
        depth = depth_of(pcs)[1]
        f32, bf16 = jnp.float32, jnp.bfloat16
        sem = pltpu.SemaphoreType.DMA
        whole = pl.BlockSpec(memory_space=pltpu.VMEM)
        dense_r, dense_c = (rows // LANES, LANES), (columns // LANES, LANES)
        shapes = (
            pltpu.VMEM(dense_r, f32), pltpu.VMEM(dense_c, f32), pltpu.VMEM((columns, programs), f32)
        )
        results = pl.pallas_call(
            functools.partial(kernel, n_src, n_tgt),
            out_shape=shapes,
            in_specs=[whole] * 3 + [pl.BlockSpec(memory_space=pl.ANY)],
            out_specs=(whole,) * 3,
            scratch_shapes=[
                pltpu.VMEM((rows, programs), bf16),
                sem(()),
                pltpu.VMEM((2, rows, width), f32),
                pltpu.VMEM((slots, depth, rows), f32),
                pltpu.VMEM((depth, columns), f32),
                pltpu.VMEM((slots, rows, depth), bf16),
                pltpu.VMEM((depth, rows), bf16),
                pltpu.VMEM((columns, depth), bf16),
                pltpu.VMEM((depth, columns), bf16),
                pltpu.VMEM((slots, programs + 16, rows), bf16),
                pltpu.VMEM((2, rows, width), bf16),
                pltpu.VMEM((2, max(rows, columns) // LANES, 8, LANES), f32),
                pltpu.VMEM((columns // width, programs + 16, width), f32),
                pltpu.VMEM((columns // width, 8, width), f32),
                pltpu.VMEM((n_src, -(-(programs + pcs) // 32) * 32, rows), f32),
                pltpu.VMEM((ITERS, n_tgt) + dense_r, f32),
                pltpu.VMEM((ITERS, n_src) + dense_c, f32),
                pltpu.VMEM((n_src,) + dense_r, f32),
                pltpu.VMEM((n_src, -(-columns // n_src // (8 * LANES)) * 8, LANES), f32),
                sem((ITERS, 2, n_tgt)),
                sem((ITERS, 2, n_tgt)),
                sem((ITERS, 2, n_src)),
                sem((ITERS, 2, n_src)),
                sem((2, n_src, 3)),
                sem((2, n_src, 3)),
                sem((2, n_src, 3)),
                sem((2, n_src, 3)),
                sem((n_src,)),
                sem((n_src,)),
                sem((columns // width + 1, 2)),
                sem((columns // width + 1, 2)),
            ],
            compiler_params=pltpu.CompilerParams(
                collective_id=0, has_side_effects=True, vmem_limit_bytes=60 * 2**20
            ),
            name="coupling",
        )(pcs_source, pcs_target, growth.reshape(dense_r), scores)
        f, g, out = pl.pallas_call(
            deliver,
            out_shape=tuple(jax.ShapeDtypeStruct(shape.shape, f32) for shape in shapes),
            in_specs=[whole] * 3,
            out_specs=(pl.BlockSpec(memory_space=pl.ANY),) * 3,
            scratch_shapes=[sem((3,))],
            name="deliver",
        )(*[pltpu.with_memory_space_constraint(result, pltpu.VMEM) for result in results])
        return f.reshape(-1), g.reshape(-1), out

    in_specs = (P(None, "src"), P(None, "tgt"), P("src"), P("src", None))
    out_specs = (P("src"), P("tgt"), P("tgt", None))
    return jax.shard_map(shards, mesh=mesh, in_specs=in_specs, out_specs=out_specs, check_vma=False)
```
